256 devices in a mesh: gx: 8 (over y, core), pa: 32 (over x, z).
Axes of the slice: x: 4, y: 4, z: 8, core: 2. Of those that a mesh axis runs over, the one named last changes fastest.
Arguments:
- u_factor: float32 [64, 65536], P(None, 'gx'), may hold values from -160 to 160, as said below
- v_factor: float32 [64, 262144], P(None, 'pa'), may hold values from -160 to 160, as said below
- mass_table: float32 [4, 16], replicated, may hold values from -2 to 2
- diffusivity_table: float32 [4, 16], replicated, may hold values from 0.2 to 1
- material_index: int32 [4, 65536], P(None, 'gx'), may hold values from 0 to 15
- band_weights: float32 [4, 3, 262144], P(None, None, 'pa'), may hold values from -5 to 5
- band_offsets: int32 [4, 3], replicated, may hold values from -4 to 4, as said below
- core_matrix: float32 [64, 64], replicated, may hold values from -4 to 4
- sketch_seed: int32 [1], replicated, may hold values from 0 to 65520
Outputs:
- u_next: float32 [64, 65536], P(None, 'gx')
- v_next: float32 [64, 262144], P(None, 'pa')
- core_next: float32 [64, 64], replicated
The draws below stay inside these ranges and needn't reach their ends.
Inputs may be any that keep to these rules, and one draw needn't show every extreme that they name: `u_factor`: each factor is finite and its rows are of mixed scales. `v_factor`: each factor is finite and its rows are of mixed scales. `band_offsets`: some tap reaches each end of the band.
All inputs are finite; a program needn't handle non-finite values.
Results may differ from the reference program's by a relative error of at most 0.0003.
Values sent between devices are 32-bit elements; how exact they have to be, the bound alone decides.
No kernel may reach another device: no remote copies, remote signals or barrier semaphores. Data moves between devices by JAX's collectives and lax.ppermute only.
A program may use at most 128 MiB of HBM per device.

```python
import math
import jax
import jax.numpy as jnp
from jax import lax

RANK = 64
STENCILS = 4
MATERIALS = 16
TAPS = 3
BAND = 4
WIDE = 256
NX = 65536
NP = 262144


def factor_draw(key, rows):
    keys = jax.random.split(key, 3)
    position = jnp.arange(rows, dtype=jnp.float32) / (rows - 1)
    rise = (1.0 + 2.0 * position)[None, :]
    column_scale = jnp.exp(jax.random.uniform(keys[2], (RANK, 1), jnp.float32, math.log(0.3), math.log(3.0)))
    base = jnp.clip(jax.random.normal(keys[0], (RANK, rows), jnp.float32), -4.0, 4.0)
    row_scale = jnp.exp(jax.random.uniform(keys[1], (1, rows), jnp.float32, 0.0, math.log(10.0)))
    return base * rise * row_scale * column_scale / 4.0


def draw_u_factor(key, part):
    return factor_draw(jax.random.fold_in(key, 101), NX)


def draw_v_factor(key, part):
    return factor_draw(jax.random.fold_in(key, 202), NP)


def draw_band_offsets(key, part):
    keys = jax.random.split(jax.random.fold_in(key, 303), 2)
    offsets = jax.random.randint(keys[0], (STENCILS, TAPS), -BAND, BAND + 1)
    picks = jax.random.randint(keys[1], (2,), 0, STENCILS)
    offsets = offsets.at[picks[0], 0].set(-BAND)
    offsets = offsets.at[picks[1], 1].set(BAND)
    return offsets.astype(jnp.int32)


def draw_core_matrix(key, part):
    keys = jax.random.split(jax.random.fold_in(key, 404), 2)
    diagonal = jax.random.uniform(keys[0], (RANK,), jnp.float32, 2.0, 4.0)
    spread = jnp.clip(0.1 * jax.random.normal(keys[1], (RANK, RANK), jnp.float32), -0.5, 0.5)
    eye = jnp.eye(RANK, dtype=jnp.float32)
    return eye * diagonal[:, None] + (1.0 - eye) * spread


def place_ends(entries, key, low, top_value):
    extent = entries.shape
    spot = [jax.random.randint(jax.random.fold_in(key, axis), (), 0, extent[axis]) for axis in range(len(extent))]
    entries = entries.at[tuple(spot)].set(low)
    longest = extent.index(max(extent))
    spot[longest] = (spot[longest] + 1) % extent[longest]
    return entries.at[tuple(spot)].set(top_value)


def levels(own_key, dims, shards, smallest, high):
    level = 1.0
    for axis_at, parts in shards:
        heights = jax.random.uniform(jax.random.fold_in(jax.random.fold_in(own_key, 6), axis_at), (parts,), jnp.float32, smallest / len(shards), high / len(shards))
        level = level * jnp.repeat(jnp.exp(heights), dims[axis_at] // parts).reshape((-1,) + (1,) * (len(dims) - 1 - axis_at))
    return level


def noise(rng, shape, deviation, reach, cuts=(), kind=jnp.bfloat16):
    entries = jax.random.normal(rng, shape, jnp.float32) * deviation
    if len(cuts) > 0:
        entries = levels(rng, shape, cuts, -0.22, 0.18) * entries
    return jnp.clip(entries, min=-reach, max=reach).astype(kind)


def setup_inputs(seed: int = 0) -> dict:
    streams_of = jax.random.split(jax.random.key(seed), 10)
    return {
        "u_factor": draw_u_factor(jax.random.fold_in(streams_of[9], 71), 0),
        "v_factor": draw_v_factor(jax.random.fold_in(streams_of[9], 71), 0),
        "mass_table": jnp.clip(jax.random.uniform(streams_of[2], (STENCILS, MATERIALS), jnp.float32, -2.0, 2.0), -2.0, 2.0),
        "diffusivity_table": jnp.clip(jnp.exp(jax.random.uniform(streams_of[3], (STENCILS, MATERIALS), jnp.float32, math.log(0.2), math.log(1.0))), 0.2, 1.0),
        "material_index": place_ends(jax.random.randint(streams_of[4], (STENCILS, NX), 0, MATERIALS), jax.random.fold_in(streams_of[4], 1), 0, MATERIALS - 1).astype(jnp.int32),
        "band_weights": noise(streams_of[5], (STENCILS, TAPS, NP), 1.0, 5.0, ((2, 32),), jnp.float32),
        "band_offsets": draw_band_offsets(jax.random.fold_in(streams_of[9], 71), 0),
        "core_matrix": draw_core_matrix(jax.random.fold_in(streams_of[9], 71), 0),
        "sketch_seed": jax.random.randint(streams_of[8], (1,), 0, 65521).astype(jnp.int32),
    }


def make_sketch(sketch_seed):
    rows_idx = lax.broadcasted_iota(jnp.int32, (WIDE, RANK), 0)
    cols_idx = lax.broadcasted_iota(jnp.int32, (WIDE, RANK), 1)
    first = (rows_idx * 131 + cols_idx * 977 + sketch_seed[0]) % 65521
    second = first * 7919 % 65521
    upper = second // 256
    lower = second % 256
    third = (upper * upper * 15 + 512 * upper * lower + lower * lower) % 65521
    fourth = (third * 30011 + rows_idx * 17 + cols_idx) % 65521
    return ((fourth.astype(jnp.float32) + 0.5) / 65521.0 - 0.5) * 3.4641

def matmul(left_m, right_m):
    return jnp.dot(left_m.astype(jnp.float32), right_m.astype(jnp.float32), precision=lax.Precision.HIGHEST, preferred_element_type=jnp.float32)

def solve_lower(lower_m, rhs, transpose):
    return lax.linalg.triangular_solve(lower_m, rhs, left_side=True, lower=True, transpose_a=transpose)

def widen_space(u_factor, mass_table, diffusivity_table, material_index):
    choices_m = jnp.arange(MATERIALS, dtype=jnp.int32)
    onehot = (material_index[:, None, :] == choices_m[None, :, None]).astype(jnp.float32)
    mass_cell = jnp.sum(mass_table[:, :, None] * onehot, axis=1)
    diffusion = jnp.sum(diffusivity_table[:, :, None] * onehot, axis=1)
    padded = jnp.pad(u_factor, ((0, 0), (1, 1)))
    laplace = padded[:, 2:] - 2.0 * u_factor + padded[:, :-2]
    blocks = mass_cell[:, None, :] * u_factor[None] + diffusion[:, None, :] * laplace[None]
    return blocks.reshape(STENCILS * RANK, u_factor.shape[1])

def widen_param(v_factor, band_weights, band_offsets):
    count = v_factor.shape[1]
    padded = jnp.pad(v_factor, ((0, 0), (BAND, BAND)))
    blocks = []
    for stencil in range(STENCILS):
        total = jnp.zeros(v_factor.shape, jnp.float32)
        for tap_index in range(TAPS):
            start = (BAND + band_offsets[stencil, tap_index]).astype(jnp.int32)
            moved = lax.dynamic_slice_in_dim(padded, start, count, 1)
            total = total + band_weights[stencil, tap_index][None, :] * moved
        blocks.append(total)
    return jnp.concatenate(blocks, axis=0)

def truncate(lower_u, lower_v, core_matrix, sketch_seed):
    block_core = jnp.kron(jnp.eye(STENCILS, dtype=jnp.float32), core_matrix)
    core_wide = matmul(matmul(lower_u.T, block_core), lower_v)
    range_y = matmul(core_wide, make_sketch(sketch_seed))
    lower_y = jnp.linalg.cholesky(matmul(range_y.T, range_y))
    left = solve_lower(lower_y, range_y.T, False).T
    back_z = matmul(core_wide.T, left)
    core_next = jnp.linalg.cholesky(matmul(back_z.T, back_z))
    right = solve_lower(core_next, back_z.T, False).T
    map_u = solve_lower(lower_u, left, True)
    map_v = solve_lower(lower_v, right, True)
    return (map_u, map_v, core_next)

def reference(u_factor, v_factor, mass_table, diffusivity_table, material_index, band_weights, band_offsets, core_matrix, sketch_seed):
    space_wide = widen_space(u_factor, mass_table, diffusivity_table, material_index)
    param_wide = widen_param(v_factor, band_weights, band_offsets)
    gram_u = matmul(space_wide, space_wide.T) / NX
    gram_v = matmul(param_wide, param_wide.T) / NP
    lower_u = jnp.linalg.cholesky(gram_u)
    lower_v = jnp.linalg.cholesky(gram_v)
    map_u, map_v, core_next = truncate(lower_u, lower_v, core_matrix, sketch_seed)
    u_next = matmul(map_u.T, space_wide)
    v_next = matmul(map_v.T, param_wide)
    return (u_next, v_next, core_next)
```

```python
import functools

import jax
import jax.numpy as jnp
from jax import lax
from jax.experimental import pallas as pl
from jax.experimental.pallas import tpu as pltpu
from jax.sharding import PartitionSpec as P

BAND = 4
LANES = 128
RANK = 64
STENCILS = 4
TAPS = 3
WIDE = 256
F32 = jnp.float32
BF16 = jnp.bfloat16
NT = (((1,), (1,)), ((), ()))
NN = (((1,), (0,)), ((), ()))
VMEM_LIMIT = 56 * 1024 * 1024


def smem():
    return pl.BlockSpec(memory_space=pltpu.SMEM)


def vmem():
    return pl.BlockSpec(memory_space=pltpu.VMEM)


def split(x):
    hi = x.astype(BF16)
    lo = (x - hi.astype(F32)).astype(BF16)
    return hi, lo


def fast_dot(a, b, dims):
    return lax.dot_general(a, b, dims, preferred_element_type=F32)


def full_dot(a, b, dims=NN):
    return lax.dot_general(a, b, dims, precision=lax.Precision.HIGHEST, preferred_element_type=F32)


def lane_iota(shape):
    return lax.broadcasted_iota(jnp.int32, shape, len(shape) - 1)


def shift_left(here, after, by):
    mask = lane_iota(here.shape) < LANES - by
    return jnp.where(mask, pltpu.roll(here, LANES - by, 1), pltpu.roll(after, LANES - by, 1))


def shift_right(before, here, by):
    mask = lane_iota(here.shape) >= by
    return jnp.where(mask, pltpu.roll(here, by, 1), pltpu.roll(before, by, 1))


def pack_gram(gram_ref, rows):
    rows[0:128, :] = gram_ref[0:128, 0:128]
    rows[128:256, :] = gram_ref[128:256, 0:128]
    rows[256:384, :] = gram_ref[128:256, 128:256]


def finish_gram(hh_ref, hl_ref, pack_ref, scale, core, mine_ref, other_ref):
    for row, col, at in ((0, 0, 0), (128, 0, 128), (128, 128, 256)):
        part = hl_ref[row:row + 128, col:col + 128] + hl_ref[col:col + 128, row:row + 128].T
        pack_ref[at:at + 128, :] = (hh_ref[row:row + 128, col:col + 128] + part) * scale
    half = 192
    mine_ref[...] = pack_ref[pl.ds(pl.multiple_of(core * half, half), half), :]
    other_ref[...] = pack_ref[pl.ds(pl.multiple_of((1 - core) * half, half), half), :]


def add_gram(hi_ref, lo_ref, hh_ref, hl_ref, first):
    hi = hi_ref[...]
    hh = fast_dot(hi, hi, NT)
    hl = fast_dot(hi, lo_ref[...], NT)

    @pl.when(first)
    def _():
        hh_ref[...] = hh
        hl_ref[...] = hl

    @pl.when(jnp.logical_not(first))
    def _():
        hh_ref[...] += hh
        hl_ref[...] += hl


def gram_scratch(tile):
    return [
        pltpu.VMEM((WIDE, tile), BF16),
        pltpu.VMEM((WIDE, tile), BF16),
        pltpu.VMEM((WIDE, WIDE), F32),
        pltpu.VMEM((WIDE, WIDE), F32),
        pltpu.VMEM((384, LANES), F32),
    ]


def gram_v_kernel(steps, scale, core_ref, off_ref, v_ref, before_ref, after_ref, halo_ref, w_ref, mine_ref, other_ref,
                  moved, hi_ref, lo_ref, hh_ref, hl_ref, pack_ref):
    step = pl.program_id(0)
    core = core_ref[0]
    tile = v_ref.shape[1]
    chunks = tile // LANES
    at_left = jnp.logical_and(step == 0, core == 0)
    at_right = jnp.logical_and(step == steps - 1, core == 1)
    before = jnp.where(at_left, halo_ref[...], before_ref[...])
    after = jnp.where(at_right, halo_ref[...], after_ref[...])
    cells = [before] + [v_ref[:, c * LANES:(c + 1) * LANES] for c in range(chunks)] + [after]
    for c in range(chunks):
        lanes = slice(c * LANES, (c + 1) * LANES)
        for by in range(1, BAND + 1):
            moved[BAND + by, :, lanes] = shift_left(cells[c + 1], cells[c + 2], by)
            moved[BAND - by, :, lanes] = shift_right(cells[c], cells[c + 1], by)
        moved[BAND, :, lanes] = cells[c + 1]
    for k in range(STENCILS):
        rows = slice(k * RANK, (k + 1) * RANK)
        for c in range(chunks):
            lanes = slice(c * LANES, (c + 1) * LANES)
            total = w_ref[k, 0:1, lanes] * moved[off_ref[k, 0] + BAND, :, lanes]
            for t in range(1, TAPS):
                total = total + w_ref[k, t:t + 1, lanes] * moved[off_ref[k, t] + BAND, :, lanes]
            hi, lo = split(total)
            hi_ref[rows, lanes] = hi
            lo_ref[rows, lanes] = lo
    add_gram(hi_ref, lo_ref, hh_ref, hl_ref, step == 0)

    @pl.when(step == steps - 1)
    def _():
        finish_gram(hh_ref, hl_ref, pack_ref, scale, core, mine_ref, other_ref)


def gram_v(core, offsets, v, halo, weights, scale):
    cells = v.shape[1]
    half = cells // 2
    tile = min(1024, half)
    steps = half // tile
    ratio = tile // LANES
    last = cells // LANES - 1
    spec = pltpu.PrefetchScalarGridSpec(
        num_scalar_prefetch=2,
        grid=(steps,),
        in_specs=[
            pl.BlockSpec((RANK, tile), lambda i, c, o: (0, c[0] * steps + i)),
            pl.BlockSpec((RANK, LANES), lambda i, c, o: (0, jnp.maximum((c[0] * steps + i) * ratio - 1, 0))),
            pl.BlockSpec((RANK, LANES), lambda i, c, o: (0, jnp.minimum((c[0] * steps + i + 1) * ratio, last))),
            pl.BlockSpec((RANK, LANES), lambda i, c, o: (0, 0)),
            pl.BlockSpec((STENCILS, TAPS, tile), lambda i, c, o: (0, 0, c[0] * steps + i)),
        ],
        out_specs=[pl.BlockSpec((192, LANES), lambda i, c, o: (0, 0))] * 2,
        scratch_shapes=[pltpu.VMEM((2 * BAND + 1, RANK, tile), F32)] + gram_scratch(tile),
    )
    return pl.pallas_call(
        functools.partial(gram_v_kernel, steps, scale),
        grid_spec=spec,
        out_shape=[jax.ShapeDtypeStruct((192, LANES), F32)] * 2,
        compiler_params=pltpu.CompilerParams(vmem_limit_bytes=VMEM_LIMIT),
        name="gram_v",
    )(core, offsets, v, v, v, halo, weights)


def ends(left_ref, before_ref, after_ref, right_ref, step, steps):
    before = jnp.where(step == 0, left_ref[...], before_ref[...])
    after = jnp.where(step == steps - 1, right_ref[...], after_ref[...])
    return before, after


def laplace_chunks(cells):
    out = []
    for c in range(1, len(cells) - 1):
        up = shift_left(cells[c], cells[c + 1], 1)
        down = shift_right(cells[c - 1], cells[c], 1)
        out.append(up - 2.0 * cells[c] + down)
    return out


def gram_u_kernel(steps, scale, core_ref, u_ref, before_ref, after_ref, left_ref, right_ref, m_ref, d_ref, mine_ref, other_ref,
                  hi_ref, lo_ref, hh_ref, hl_ref, pack_ref):
    step = pl.program_id(0)
    chunks = u_ref.shape[1] // LANES
    before, after = ends(left_ref, before_ref, after_ref, right_ref, step, steps)
    cells = [before] + [u_ref[:, c * LANES:(c + 1) * LANES] for c in range(chunks)] + [after]
    laps = laplace_chunks(cells)
    for c in range(chunks):
        lanes = slice(c * LANES, (c + 1) * LANES)
        for k in range(STENCILS):
            rows = slice(k * RANK, (k + 1) * RANK)
            total = m_ref[k:k + 1, lanes] * cells[c + 1] + d_ref[k:k + 1, lanes] * laps[c]
            hi, lo = split(total)
            hi_ref[rows, lanes] = hi
            lo_ref[rows, lanes] = lo
    add_gram(hi_ref, lo_ref, hh_ref, hl_ref, step == 0)

    @pl.when(step == steps - 1)
    def _():
        finish_gram(hh_ref, hl_ref, pack_ref, scale, core_ref[0], mine_ref, other_ref)


def tile_specs(tile, cells):
    ratio = tile // LANES
    last = cells // LANES - 1
    return [
        pl.BlockSpec((RANK, tile), lambda i, *_: (0, i)),
        pl.BlockSpec((RANK, LANES), lambda i, *_: (0, jnp.maximum(i * ratio - 1, 0))),
        pl.BlockSpec((RANK, LANES), lambda i, *_: (0, jnp.minimum((i + 1) * ratio, last))),
        pl.BlockSpec((RANK, LANES), lambda i, *_: (0, 0)),
        pl.BlockSpec((RANK, LANES), lambda i, *_: (0, 0)),
    ]


def gram_u(core, u, left, right, mass, diffusion, scale):
    cells = u.shape[1]
    tile = min(1024, cells)
    steps = cells // tile
    table = pl.BlockSpec((STENCILS, tile), lambda i, *_: (0, i))
    spec = pltpu.PrefetchScalarGridSpec(
        num_scalar_prefetch=1,
        grid=(steps,),
        in_specs=tile_specs(tile, cells) + [table, table],
        out_specs=[pl.BlockSpec((192, LANES), lambda i, *_: (0, 0))] * 2,
        scratch_shapes=gram_scratch(tile),
    )
    return pl.pallas_call(
        functools.partial(gram_u_kernel, steps, scale),
        grid_spec=spec,
        out_shape=[jax.ShapeDtypeStruct((192, LANES), F32)] * 2,
        compiler_params=pltpu.CompilerParams(vmem_limit_bytes=VMEM_LIMIT),
        name="gram_u",
    )(core, u, u, u, left, right, mass, diffusion)


def lower_inverse(square):
    size = RANK
    groups = size // 8
    rows_idx = lax.broadcasted_iota(jnp.int32, (size, size), 0)
    cols_idx = lax.broadcasted_iota(jnp.int32, (size, size), 1)
    unit = jnp.where(rows_idx == cols_idx, 1.0, 0.0).astype(F32)
    both = jnp.concatenate([square, unit], axis=1)
    work = [both[8 * q:8 * q + 8, :] for q in range(groups)]
    shape = (8, 2 * size)
    sub = lax.broadcasted_iota(jnp.int32, shape, 0)
    done = []
    for p in range(groups):
        cols = [[jnp.broadcast_to(work[q][:, 8 * p + j:8 * p + j + 1], shape) for q in range(p, groups)] for j in range(8)]
        rows = [jnp.broadcast_to(work[p][j:j + 1, :], shape) for j in range(8)]
        scaled = []
        kept = None
        for j in range(8):
            pivot = jnp.broadcast_to(cols[j][0][j:j + 1, :], shape)
            inv = 1.0 / pivot
            for k in range(j + 1, 8):
                factor = jnp.broadcast_to(cols[j][0][k:k + 1, :], shape) * inv
                for q in range(groups - p):
                    cols[k][q] = cols[k][q] - cols[j][q] * factor
                rows[k] = rows[k] - rows[j] * factor
            scaled.append(rows[j] * inv)
            unit_row = rows[j] * lax.rsqrt(pivot)
            kept = unit_row if j == 0 else jnp.where(sub == j, unit_row, kept)
        for q in range(p + 1, groups):
            for j in range(8):
                work[q] = work[q] - cols[j][q - p] * scaled[j]
        done.append(kept)
    return jnp.concatenate(done, axis=0)[:, size:]


def unpack(core, mine_ref, other_ref, full_ref):
    first = core == 0
    low = jnp.where(first, mine_ref[...], other_ref[...])
    high = jnp.where(first, other_ref[...], mine_ref[...])
    g10 = jnp.concatenate([low[128:192], high[0:64]], axis=0)
    full_ref[0:128, 0:128] = low[0:128]
    full_ref[128:256, 0:128] = g10
    full_ref[0:128, 128:256] = g10.T
    full_ref[128:256, 128:256] = high[64:192]


def three(x):
    hi, lo = split(x)
    return jnp.concatenate([hi, hi, lo], axis=1)


def chain_kernel(core_ref, gv_mine, gv_other, gu_mine, gu_other, sketch_ref, c_ref, mu_ref, mv_ref, next_ref,
                 gv_ref, gu_ref, panel_ref, block_ref):
    core = core_ref[0]
    unpack(core, gv_mine, gv_other, gv_ref)
    unpack(core, gu_mine, gu_other, gu_ref)
    block_ref[...] = jnp.zeros_like(block_ref)
    for k in range(STENCILS):
        at = slice(k * RANK, (k + 1) * RANK)
        block_ref[at, at] = c_ref[...]
        panel_ref[k] = gv_ref[:, at]
    parts = [None] * STENCILS
    for p in range(STENCILS):
        at = slice(p * RANK, (p + 1) * RANK)
        inverse = lower_inverse(panel_ref[p, at, :])
        below = full_dot(panel_ref[p, p * RANK:, :], inverse, NT)
        for q in range(p + 1, STENCILS):
            head = (q - p) * RANK
            panel_ref[q, q * RANK:, :] -= full_dot(below[head:], below[head:head + RANK], NT)
        for q in range(p, STENCILS):
            head = (q - p) * RANK
            block = below[head:head + RANK]
            if q == p:
                block = jnp.where(
                    lax.broadcasted_iota(jnp.int32, block.shape, 0) >= lane_iota(block.shape), block, 0.0)
            term = full_dot(sketch_ref[p], block, NT)
            parts[q] = term if parts[q] is None else parts[q] + term
    base = jnp.concatenate(parts, axis=1)
    w_t = full_dot(base, block_ref[...], NT)
    k_t = full_dot(w_t, gu_ref[...])
    inverse_y = lower_inverse(full_dot(w_t, k_t, NT))
    x_t = full_dot(inverse_y, full_dot(k_t, block_ref[...]))
    map_u = full_dot(inverse_y, w_t)
    inner = full_dot(x_t, full_dot(x_t, gv_ref[...]), NT)
    inverse_c = lower_inverse(inner)
    map_v = full_dot(inverse_c, x_t)
    lower = full_dot(inner, inverse_c, NT)
    keep = lax.broadcasted_iota(jnp.int32, lower.shape, 0) >= lane_iota(lower.shape)
    next_ref[...] = jnp.where(keep, lower, 0.0)
    for k in range(STENCILS):
        at = slice(k * RANK, (k + 1) * RANK)
        mu_ref[at, :] = three(map_u[:, at])
        mv_ref[at, :] = three(map_v[:, at])


def chain(core, gv_mine, gv_other, gu_mine, gu_other, sketch_t, core_matrix):
    return pl.pallas_call(
        chain_kernel,
        in_specs=[smem()] + [vmem()] * 6,
        out_specs=[vmem()] * 3,
        out_shape=[
            jax.ShapeDtypeStruct((WIDE, 3 * RANK), BF16),
            jax.ShapeDtypeStruct((WIDE, 3 * RANK), BF16),
            jax.ShapeDtypeStruct((RANK, RANK), F32),
        ],
        scratch_shapes=[
            pltpu.VMEM((WIDE, WIDE), F32),
            pltpu.VMEM((WIDE, WIDE), F32),
            pltpu.VMEM((STENCILS, WIDE, RANK), F32),
            pltpu.VMEM((WIDE, WIDE), F32),
        ],
        compiler_params=pltpu.CompilerParams(vmem_limit_bytes=VMEM_LIMIT),
        name="chain",
    )(core, gv_mine, gv_other, gu_mine, gu_other, sketch_t, core_matrix)


def put_three(ref, at, x):
    hi, lo = split(x)
    ref[0:RANK, at] = hi
    ref[RANK:2 * RANK, at] = lo
    ref[2 * RANK:3 * RANK, at] = hi


def next_u_kernel(steps, u_ref, before_ref, after_ref, left_ref, right_ref, m_ref, d_ref, map_ref, out_ref, plain, laps, p_ref, q_ref):
    step = pl.program_id(0)
    chunks = u_ref.shape[1] // LANES
    before, after = ends(left_ref, before_ref, after_ref, right_ref, step, steps)
    cells = [before] + [u_ref[:, c * LANES:(c + 1) * LANES] for c in range(chunks)] + [after]
    second = laplace_chunks(cells)
    for c in range(chunks):
        at = slice(c * LANES, (c + 1) * LANES)
        put_three(plain, at, cells[c + 1])
        put_three(laps, at, second[c])
    p_ref[...] = fast_dot(map_ref[...], plain[...], NN)
    q_ref[...] = fast_dot(map_ref[...], laps[...], NN)
    for c in range(chunks):
        at = slice(c * LANES, (c + 1) * LANES)
        total = None
        for k in range(STENCILS):
            rows = slice(k * RANK, (k + 1) * RANK)
            term = m_ref[k:k + 1, at] * p_ref[rows, at] + d_ref[k:k + 1, at] * q_ref[rows, at]
            total = term if total is None else total + term
        out_ref[:, at] = total


def next_u(u, left, right, mass, diffusion, map_u):
    cells = u.shape[1]
    tile = min(1024, cells)
    steps = cells // tile
    table = pl.BlockSpec((STENCILS, tile), lambda i: (0, i))
    return pl.pallas_call(
        functools.partial(next_u_kernel, steps),
        grid=(steps,),
        in_specs=tile_specs(tile, cells) + [table, table, pl.BlockSpec((WIDE, 3 * RANK), lambda i: (0, 0))],
        out_specs=pl.BlockSpec((RANK, tile), lambda i: (0, i)),
        out_shape=jax.ShapeDtypeStruct((RANK, cells), F32),
        scratch_shapes=[pltpu.VMEM((3 * RANK, tile), BF16)] * 2 + [pltpu.VMEM((WIDE, tile), F32)] * 2,
        compiler_params=pltpu.CompilerParams(vmem_limit_bytes=VMEM_LIMIT),
        name="next_u",
    )(u, u, u, left, right, mass, diffusion, map_u)


def next_v_kernel(steps, off_ref, v_ref, before_ref, after_ref, left_ref, right_ref, w_ref, map_ref, out_ref, plain, p_ref):
    step = pl.program_id(0)
    chunks = v_ref.shape[1] // LANES
    before, after = ends(left_ref, before_ref, after_ref, right_ref, step, steps)
    cells = [before] + [v_ref[:, c * LANES:(c + 1) * LANES] for c in range(chunks)] + [after]
    for c in range(chunks + 2):
        put_three(plain, slice(c * LANES, (c + 1) * LANES), cells[c])
    p_ref[...] = fast_dot(map_ref[...], plain[...], NN)
    lane = lane_iota((RANK, LANES))
    for k in range(STENCILS):
        rows = slice(k * RANK, (k + 1) * RANK)
        for t in range(TAPS):
            by = off_ref[k, t]
            turn = lax.rem(LANES - by, LANES)
            near = jnp.where(by >= 0, 1, -1)
            inside = jnp.logical_and(lane + by >= 0, lane + by < LANES)
            for c in range(chunks):
                at = slice(c * LANES, (c + 1) * LANES)
                here = p_ref[rows, (c + 1) * LANES:(c + 2) * LANES]
                there = p_ref[rows, pl.ds(pl.multiple_of((c + 1 + near) * LANES, LANES), LANES)]
                mixed = jnp.where(inside, pltpu.roll(here, turn, 1), pltpu.roll(there, turn, 1))
                term = w_ref[k, t:t + 1, at] * mixed
                if k == 0 and t == 0:
                    out_ref[:, at] = term
                else:
                    out_ref[:, at] += term


def next_v(offsets, v, left, right, weights, map_v):
    cells = v.shape[1]
    tile = min(1024, cells)
    steps = cells // tile
    spec = pltpu.PrefetchScalarGridSpec(
        num_scalar_prefetch=1,
        grid=(steps,),
        in_specs=tile_specs(tile, cells) + [
            pl.BlockSpec((STENCILS, TAPS, tile), lambda i, *_: (0, 0, i)),
            pl.BlockSpec((WIDE, 3 * RANK), lambda i, *_: (0, 0)),
        ],
        out_specs=pl.BlockSpec((RANK, tile), lambda i, *_: (0, i)),
        scratch_shapes=[pltpu.VMEM((3 * RANK, tile + 2 * LANES), BF16), pltpu.VMEM((WIDE, tile + 2 * LANES), F32)],
    )
    return pl.pallas_call(
        functools.partial(next_v_kernel, steps),
        grid_spec=spec,
        out_shape=jax.ShapeDtypeStruct((RANK, cells), F32),
        compiler_params=pltpu.CompilerParams(vmem_limit_bytes=VMEM_LIMIT),
        name="next_v",
    )(offsets, v, v, v, left, right, weights, map_v)


def make_sketch_t(sketch_seed, wide, rank):
    shape = (wide // rank, rank, rank)
    rows_idx = lax.broadcasted_iota(jnp.int32, shape, 0) * rank + lax.broadcasted_iota(jnp.int32, shape, 2)
    cols_idx = lax.broadcasted_iota(jnp.int32, shape, 1)
    first = (rows_idx * 131 + cols_idx * 977 + sketch_seed[0]) % 65521
    second = first * 7919 % 65521
    upper = second // 256
    lower = second % 256
    third = (upper * upper * 15 + 512 * upper * lower + lower * lower) % 65521
    fourth = (third * 30011 + rows_idx * 17 + cols_idx) % 65521
    return ((fourth.astype(F32) + 0.5) / 65521.0 - 0.5) * 3.4641


def swap(x, axis, bit):
    return lax.ppermute(x, axis, [(i, i ^ bit) for i in range(lax.axis_size(axis))])


def local(u, v, mass_table, diffusivity_table, material_index, weights, offsets, core_matrix, sketch_seed):
    gx, pa = lax.axis_size("gx"), lax.axis_size("pa")
    at_gx = lax.axis_index("gx")
    core = (at_gx % 2).astype(jnp.int32).reshape(1)
    even = core[0] == 0
    head, tail = v[:, :LANES], v[:, -LANES:]
    send = jnp.where(even, tail, head)
    pairs = []
    for g in range(gx):
        for p in range(pa):
            q = p + 1 if g % 2 == 0 else p - 1
            if 0 <= q < pa:
                pairs.append((g * pa + p, g * pa + q))
    halo = lax.ppermute(send, ("gx", "pa"), pairs)
    gv_mine, gv_other = gram_v(core, offsets, v, halo, weights, 1.0 / (v.shape[1] * pa))

    halo_other = swap(halo, "gx", 1)
    left_v = jnp.where(even, halo, halo_other)
    right_v = jnp.where(even, halo_other, halo)
    left_u = lax.ppermute(u[:, -LANES:], "gx", [(i, i + 1) for i in range(gx - 1)])
    right_u = lax.ppermute(u[:, :LANES], "gx", [(i + 1, i) for i in range(gx - 1)])
    onehot = (material_index[:, None, :] == jnp.arange(mass_table.shape[1], dtype=jnp.int32)[None, :, None]).astype(F32)
    mass = jnp.sum(mass_table[:, :, None] * onehot, axis=1)
    diffusion = jnp.sum(diffusivity_table[:, :, None] * onehot, axis=1)
    gu_mine, gu_other = gram_u(core, u, left_u, right_u, mass, diffusion, 1.0 / (u.shape[1] * gx))

    gv = gv_mine + swap(gv_other, "gx", 1)
    bit = 1
    while bit < pa:
        gv = gv + swap(gv, "pa", bit)
        bit *= 2
    gu = gu_mine + swap(gu_other, "gx", 1)
    bit = 2
    while bit < gx:
        gu = gu + swap(gu, "gx", bit)
        bit *= 2
    gv_far = swap(gv, "gx", 1)
    gu_far = swap(gu, "gx", 1)
    sketch_t = make_sketch_t(sketch_seed, WIDE, RANK)
    map_u, map_v, core_next = chain(core, gv, gv_far, gu, gu_far, sketch_t, core_matrix)
    u_next = next_u(u, left_u, right_u, mass, diffusion, map_u)
    v_next = next_v(offsets, v, left_v, right_v, weights, map_v)
    return (u_next, v_next, core_next)


def solution(mesh):
    return jax.shard_map(
        local,
        mesh=mesh,
        in_specs=(
            P(None, "gx"),
            P(None, "pa"),
            P(),
            P(),
            P(None, "gx"),
            P(None, None, "pa"),
            P(),
            P(),
            P(),
        ),
        out_specs=(P(None, "gx"), P(None, "pa"), P()),
        check_vma=False,
    )
```

```python
import functools

import jax
import jax.numpy as jnp
from jax import lax
from jax.experimental import pallas as pl
from jax.experimental.pallas import tpu as pltpu
from jax.sharding import PartitionSpec as P

BAND = 4
LANES = 128
RANK = 64
STENCILS = 4
TAPS = 3
WIDE = 256
F32 = jnp.float32
BF16 = jnp.bfloat16
NT = (((1,), (1,)), ((), ()))
NN = (((1,), (0,)), ((), ()))
VMEM_LIMIT = 56 * 1024 * 1024


def smem():
    return pl.BlockSpec(memory_space=pltpu.SMEM)


def vmem():
    return pl.BlockSpec(memory_space=pltpu.VMEM)


def split(x):
    hi = x.astype(BF16)
    lo = (x - hi.astype(F32)).astype(BF16)
    return hi, lo


def fast_dot(a, b, dims):
    return lax.dot_general(a, b, dims, preferred_element_type=F32)


def full_dot(a, b, dims=NN):
    return lax.dot_general(a, b, dims, precision=lax.Precision.HIGHEST, preferred_element_type=F32)


def lane_iota(shape):
    return lax.broadcasted_iota(jnp.int32, shape, len(shape) - 1)


def shift_left(here, after, by):
    mask = lane_iota(here.shape) < LANES - by
    return jnp.where(mask, pltpu.roll(here, LANES - by, 1), pltpu.roll(after, LANES - by, 1))


def shift_right(before, here, by):
    mask = lane_iota(here.shape) >= by
    return jnp.where(mask, pltpu.roll(here, by, 1), pltpu.roll(before, by, 1))


def finish_gram(hh_ref, hl_ref, pack_ref, scale, core, mine_ref, other_ref):
    for row, col, at in ((0, 0, 0), (128, 0, 128), (128, 128, 256)):
        part = hl_ref[row:row + 128, col:col + 128] + hl_ref[col:col + 128, row:row + 128].T
        pack_ref[at:at + 128, :] = (hh_ref[row:row + 128, col:col + 128] + part) * scale
    half = 192
    mine_ref[...] = pack_ref[pl.ds(pl.multiple_of(core * half, half), half), :]
    other_ref[...] = pack_ref[pl.ds(pl.multiple_of((1 - core) * half, half), half), :]


def add_gram(hi_ref, lo_ref, hh_ref, hl_ref):
    hi = hi_ref[...]
    hh_ref[...] += fast_dot(hi, hi, NT)
    hl_ref[...] += fast_dot(hi, lo_ref[...], NT)


def keep_wide(total, k, near, at, hi_ref, lo_ref, wide_hi, wide_lo):
    rows = slice(k * RANK, (k + 1) * RANK)
    hi, lo = split(total)
    hi_ref[rows, near] = hi
    lo_ref[rows, near] = lo
    wide_hi[rows, at] = hi
    wide_lo[rows, at] = lo


def gram_scratch(part):
    return [pltpu.VMEM((WIDE, part), BF16)] * 4 + [pltpu.VMEM((WIDE, WIDE), F32)] * 2 + [pltpu.VMEM((384, LANES), F32)]


def start_gram(hi_ref, lo_ref, hh_ref, hl_ref):
    hi_ref[...] = jnp.zeros_like(hi_ref)
    lo_ref[...] = jnp.zeros_like(lo_ref)
    hh_ref[...] = jnp.zeros_like(hh_ref)
    hl_ref[...] = jnp.zeros_like(hl_ref)


def shift_all(cells, first, count, moved):
    for i in range(count):
        c = first + i
        lanes = slice(i * LANES, (i + 1) * LANES)
        for by in range(1, BAND + 1):
            moved[BAND + by, :, lanes] = shift_left(cells[c + 1], cells[c + 2], by)
            moved[BAND - by, :, lanes] = shift_right(cells[c], cells[c + 1], by)
        moved[BAND, :, lanes] = cells[c + 1]


def gram_v_kernel(steps, scale, core_ref, off_ref, v_ref, before_ref, after_ref, halo_ref, w_ref,
                  mine_ref, other_ref, wide_hi, wide_lo,
                  moved_a, moved_b, hi_a, lo_a, hi_b, lo_b, hh_ref, hl_ref, pack_ref):
    step = pl.program_id(0)
    core = core_ref[0]
    tile = v_ref.shape[1]
    chunks = tile // LANES
    part = chunks // 2

    @pl.when(step == 0)
    def _():
        start_gram(hi_b, lo_b, hh_ref, hl_ref)

    at_left = jnp.logical_and(step == 0, core == 0)
    at_right = jnp.logical_and(step == steps - 1, core == 1)
    before = jnp.where(at_left, halo_ref[...], before_ref[...])
    after = jnp.where(at_right, halo_ref[...], after_ref[...])
    cells = [before] + [v_ref[:, c * LANES:(c + 1) * LANES] for c in range(chunks)] + [after]
    add_gram(hi_b, lo_b, hh_ref, hl_ref)
    for half, moved, hi_ref, lo_ref in ((0, moved_a, hi_a, lo_a), (1, moved_b, hi_b, lo_b)):
        shift_all(cells, half * part, part, moved)
        for k in range(STENCILS):
            for i in range(part):
                near = slice(i * LANES, (i + 1) * LANES)
                at = slice((half * part + i) * LANES, (half * part + i + 1) * LANES)
                total = w_ref[0, k:k + 1, at] * moved[off_ref[k, 0] + BAND, :, near]
                for t in range(1, TAPS):
                    total = total + w_ref[t, k:k + 1, at] * moved[off_ref[k, t] + BAND, :, near]
                keep_wide(total, k, near, at, hi_ref, lo_ref, wide_hi, wide_lo)
        if half == 0:
            add_gram(hi_a, lo_a, hh_ref, hl_ref)

    @pl.when(step == steps - 1)
    def _():
        add_gram(hi_b, lo_b, hh_ref, hl_ref)
        finish_gram(hh_ref, hl_ref, pack_ref, scale, core, mine_ref, other_ref)


def gram_v(core, offsets, v, halo, weights, scale):
    cells = v.shape[1]
    half = cells // 2
    tile = min(1024, half)
    steps = half // tile
    ratio = tile // LANES
    last = cells // LANES - 1
    spec = pltpu.PrefetchScalarGridSpec(
        num_scalar_prefetch=2,
        grid=(steps,),
        in_specs=[
            pl.BlockSpec((RANK, tile), lambda i, c, o: (0, c[0] * steps + i)),
            pl.BlockSpec((RANK, LANES), lambda i, c, o: (0, jnp.maximum((c[0] * steps + i) * ratio - 1, 0))),
            pl.BlockSpec((RANK, LANES), lambda i, c, o: (0, jnp.minimum((c[0] * steps + i + 1) * ratio, last))),
            pl.BlockSpec((RANK, LANES), lambda i, c, o: (0, 0)),
            pl.BlockSpec((TAPS, STENCILS, tile), lambda i, c, o: (0, 0, c[0] * steps + i)),
        ],
        out_specs=[pl.BlockSpec((192, LANES), lambda i, c, o: (0, 0))] * 2 + [pl.BlockSpec((WIDE, tile), lambda i, c, o: (0, i))] * 2,
        scratch_shapes=[pltpu.VMEM((2 * BAND + 1, RANK, tile // 2), F32)] * 2 + gram_scratch(tile // 2),
    )
    return pl.pallas_call(
        functools.partial(gram_v_kernel, steps, scale),
        grid_spec=spec,
        out_shape=[jax.ShapeDtypeStruct((192, LANES), F32)] * 2 + [jax.ShapeDtypeStruct((WIDE, half), BF16)] * 2,
        compiler_params=pltpu.CompilerParams(vmem_limit_bytes=VMEM_LIMIT),
        name="gram_v",
    )(core, offsets, v, v, v, halo, weights)


def gram_u_kernel(steps, scale, core_ref, u_ref, before_ref, after_ref, left_ref, right_ref, m_ref, d_ref,
                  mine_ref, other_ref, wide_hi, wide_lo,
                  hi_a, lo_a, hi_b, lo_b, hh_ref, hl_ref, pack_ref):
    step = pl.program_id(0)
    chunks = u_ref.shape[1] // LANES
    part = chunks // 2

    @pl.when(step == 0)
    def _():
        start_gram(hi_b, lo_b, hh_ref, hl_ref)

    before = jnp.where(step == 0, left_ref[...], before_ref[...])
    after = jnp.where(step == steps - 1, right_ref[...], after_ref[...])
    cells = [before] + [u_ref[:, c * LANES:(c + 1) * LANES] for c in range(chunks)] + [after]
    add_gram(hi_b, lo_b, hh_ref, hl_ref)
    for half, hi_ref, lo_ref in ((0, hi_a, lo_a), (1, hi_b, lo_b)):
        for i in range(part):
            c = half * part + i
            near = slice(i * LANES, (i + 1) * LANES)
            at = slice(c * LANES, (c + 1) * LANES)
            up = shift_left(cells[c + 1], cells[c + 2], 1)
            down = shift_right(cells[c], cells[c + 1], 1)
            lap = up - 2.0 * cells[c + 1] + down
            for k in range(STENCILS):
                total = m_ref[k:k + 1, at] * cells[c + 1] + d_ref[k:k + 1, at] * lap
                keep_wide(total, k, near, at, hi_ref, lo_ref, wide_hi, wide_lo)
        if half == 0:
            add_gram(hi_a, lo_a, hh_ref, hl_ref)

    @pl.when(step == steps - 1)
    def _():
        add_gram(hi_b, lo_b, hh_ref, hl_ref)
        finish_gram(hh_ref, hl_ref, pack_ref, scale, core_ref[0], mine_ref, other_ref)


def gram_u(core, u, left, right, mass, diffusion, scale):
    cells = u.shape[1]
    tile = min(1024, cells)
    steps = cells // tile
    ratio = tile // LANES
    last = cells // LANES - 1
    table = pl.BlockSpec((STENCILS, tile), lambda i, *_: (0, i))
    spec = pltpu.PrefetchScalarGridSpec(
        num_scalar_prefetch=1,
        grid=(steps,),
        in_specs=[
            pl.BlockSpec((RANK, tile), lambda i, *_: (0, i)),
            pl.BlockSpec((RANK, LANES), lambda i, *_: (0, jnp.maximum(i * ratio - 1, 0))),
            pl.BlockSpec((RANK, LANES), lambda i, *_: (0, jnp.minimum((i + 1) * ratio, last))),
            pl.BlockSpec((RANK, LANES), lambda i, *_: (0, 0)),
            pl.BlockSpec((RANK, LANES), lambda i, *_: (0, 0)),
            table,
            table,
        ],
        out_specs=[pl.BlockSpec((192, LANES), lambda i, *_: (0, 0))] * 2 + [pl.BlockSpec((WIDE, tile), lambda i, *_: (0, i))] * 2,
        scratch_shapes=gram_scratch(tile // 2),
    )
    return pl.pallas_call(
        functools.partial(gram_u_kernel, steps, scale),
        grid_spec=spec,
        out_shape=[jax.ShapeDtypeStruct((192, LANES), F32)] * 2 + [jax.ShapeDtypeStruct((WIDE, cells), BF16)] * 2,
        compiler_params=pltpu.CompilerParams(vmem_limit_bytes=VMEM_LIMIT),
        name="gram_u",
    )(core, u, u, u, left, right, mass, diffusion)


def lower_inverse(square):
    size = RANK
    groups = size // 8
    rows_idx = lax.broadcasted_iota(jnp.int32, (size, size), 0)
    cols_idx = lax.broadcasted_iota(jnp.int32, (size, size), 1)
    unit = jnp.where(rows_idx == cols_idx, 1.0, 0.0).astype(F32)
    both = jnp.concatenate([square, unit], axis=1)
    work = [both[8 * q:8 * q + 8, :] for q in range(groups)]
    shape = (8, 2 * size)
    sub = lax.broadcasted_iota(jnp.int32, shape, 0)
    done = []
    for p in range(groups):
        cols = [[jnp.broadcast_to(work[q][:, 8 * p + j:8 * p + j + 1], shape) for q in range(p, groups)] for j in range(8)]
        rows = [jnp.broadcast_to(work[p][j:j + 1, :], shape) for j in range(8)]
        scaled = []
        kept = None
        for j in range(8):
            pivot = jnp.broadcast_to(cols[j][0][j:j + 1, :], shape)
            inv = 1.0 / pivot
            for k in range(j + 1, 8):
                factor = jnp.broadcast_to(cols[j][0][k:k + 1, :], shape) * inv
                for q in range(groups - p):
                    cols[k][q] = cols[k][q] - cols[j][q] * factor
                rows[k] = rows[k] - rows[j] * factor
            scaled.append(rows[j] * inv)
            unit_row = rows[j] * lax.rsqrt(pivot)
            kept = unit_row if j == 0 else jnp.where(sub == j, unit_row, kept)
        for q in range(p + 1, groups):
            for j in range(8):
                work[q] = work[q] - cols[j][q - p] * scaled[j]
        done.append(kept)
    return jnp.concatenate(done, axis=0)[:, size:]


def unpack(core, mine_ref, other_ref, full_ref):
    first = core == 0
    low = jnp.where(first, mine_ref[...], other_ref[...])
    high = jnp.where(first, other_ref[...], mine_ref[...])
    g10 = jnp.concatenate([low[128:192], high[0:64]], axis=0)
    full_ref[0:128, 0:128] = low[0:128]
    full_ref[128:256, 0:128] = g10
    full_ref[0:128, 128:256] = g10.T
    full_ref[128:256, 128:256] = high[64:192]


def put_split(ref, x):
    hi, lo = split(x)
    ref[0:RANK, :] = hi
    ref[RANK:2 * RANK, :] = lo


def chain_kernel(core_ref, gv_mine, gv_other, gu_mine, gu_other, sketch_ref, c_ref, mu_ref, mv_ref, next_ref,
                 gv_ref, gu_ref, panel_ref, block_ref):
    core = core_ref[0]
    unpack(core, gv_mine, gv_other, gv_ref)
    unpack(core, gu_mine, gu_other, gu_ref)
    block_ref[...] = jnp.zeros_like(block_ref)
    for k in range(STENCILS):
        at = slice(k * RANK, (k + 1) * RANK)
        block_ref[at, at] = c_ref[...]
        panel_ref[k] = gv_ref[:, at]
    parts = [None] * STENCILS
    for p in range(STENCILS):
        at = slice(p * RANK, (p + 1) * RANK)
        inverse = lower_inverse(panel_ref[p, at, :])
        below = full_dot(panel_ref[p, p * RANK:, :], inverse, NT)
        for q in range(p + 1, STENCILS):
            head = (q - p) * RANK
            panel_ref[q, q * RANK:, :] -= full_dot(below[head:], below[head:head + RANK], NT)
        for q in range(p, STENCILS):
            head = (q - p) * RANK
            block = below[head:head + RANK]
            if q == p:
                block = jnp.where(
                    lax.broadcasted_iota(jnp.int32, block.shape, 0) >= lane_iota(block.shape), block, 0.0)
            term = full_dot(sketch_ref[p], block, NT)
            parts[q] = term if parts[q] is None else parts[q] + term
    base = jnp.concatenate(parts, axis=1)
    w_t = full_dot(base, block_ref[...], NT)
    k_t = full_dot(w_t, gu_ref[...])
    inverse_y = lower_inverse(full_dot(w_t, k_t, NT))
    x_t = full_dot(inverse_y, full_dot(k_t, block_ref[...]))
    map_u = full_dot(inverse_y, w_t)
    inner = full_dot(x_t, full_dot(x_t, gv_ref[...]), NT)
    inverse_c = lower_inverse(inner)
    map_v = full_dot(inverse_c, x_t)
    lower = full_dot(inner, inverse_c, NT)
    keep = lax.broadcasted_iota(jnp.int32, lower.shape, 0) >= lane_iota(lower.shape)
    next_ref[...] = jnp.where(keep, lower, 0.0)
    put_split(mu_ref, map_u)
    put_split(mv_ref, map_v)


def chain(core, gv_mine, gv_other, gu_mine, gu_other, sketch_t, core_matrix):
    return pl.pallas_call(
        chain_kernel,
        in_specs=[smem()] + [vmem()] * 6,
        out_specs=[vmem()] * 3,
        out_shape=[
            jax.ShapeDtypeStruct((2 * RANK, WIDE), BF16),
            jax.ShapeDtypeStruct((2 * RANK, WIDE), BF16),
            jax.ShapeDtypeStruct((RANK, RANK), F32),
        ],
        scratch_shapes=[
            pltpu.VMEM((WIDE, WIDE), F32),
            pltpu.VMEM((WIDE, WIDE), F32),
            pltpu.VMEM((STENCILS, WIDE, RANK), F32),
            pltpu.VMEM((WIDE, WIDE), F32),
        ],
        compiler_params=pltpu.CompilerParams(vmem_limit_bytes=VMEM_LIMIT),
        name="chain",
    )(core, gv_mine, gv_other, gu_mine, gu_other, sketch_t, core_matrix)


def next_kernel(map_ref, hi_ref, lo_ref, out_ref):
    both = fast_dot(map_ref[...], hi_ref[...], NN)
    out_ref[...] = both[0:RANK] + (both[RANK:2 * RANK] + fast_dot(map_ref[0:RANK, :], lo_ref[...], NN))


def next_factor(name, maps, wide_hi, wide_lo):
    cells = wide_hi.shape[1]
    tile = min(1024, cells)
    return pl.pallas_call(
        next_kernel,
        grid=(cells // tile,),
        in_specs=[
            pl.BlockSpec((2 * RANK, WIDE), lambda i: (0, 0)),
            pl.BlockSpec((WIDE, tile), lambda i: (0, i)),
            pl.BlockSpec((WIDE, tile), lambda i: (0, i)),
        ],
        out_specs=pl.BlockSpec((RANK, tile), lambda i: (0, i)),
        out_shape=jax.ShapeDtypeStruct((RANK, cells), F32),
        compiler_params=pltpu.CompilerParams(vmem_limit_bytes=VMEM_LIMIT),
        name=name,
    )(maps, wide_hi, wide_lo)


def make_sketch_t(sketch_seed, wide, rank):
    shape = (wide // rank, rank, rank)
    rows_idx = lax.broadcasted_iota(jnp.int32, shape, 0) * rank + lax.broadcasted_iota(jnp.int32, shape, 2)
    cols_idx = lax.broadcasted_iota(jnp.int32, shape, 1)
    first = (rows_idx * 131 + cols_idx * 977 + sketch_seed[0]) % 65521
    second = first * 7919 % 65521
    upper = second // 256
    lower = second % 256
    third = (upper * upper * 15 + 512 * upper * lower + lower * lower) % 65521
    fourth = (third * 30011 + rows_idx * 17 + cols_idx) % 65521
    return ((fourth.astype(F32) + 0.5) / 65521.0 - 0.5) * 3.4641


def swap(x, axis, bit):
    return lax.ppermute(x, axis, [(i, i ^ bit) for i in range(lax.axis_size(axis))])


def local(u, v, mass_table, diffusivity_table, material_index, weights, offsets, core_matrix, sketch_seed):
    gx, pa = lax.axis_size("gx"), lax.axis_size("pa")
    at_gx = lax.axis_index("gx")
    core = (at_gx % 2).astype(jnp.int32).reshape(1)
    even = core[0] == 0
    at_pa = lax.axis_index("pa")
    edge_u = jnp.where(even, u[:, :LANES], u[:, -LANES:])
    edge_v = jnp.where(even, v[:, :LANES], v[:, -LANES:])
    pairs = []
    for g in range(gx):
        for p in range(pa):
            if g % 2 == 0:
                pairs.append((g * pa + p, (g - 1) % gx * pa + (p - 1) % pa))
            else:
                pairs.append((g * pa + p, (g + 1) % gx * pa + (p + 1) % pa))
    far = lax.ppermute(jnp.concatenate([edge_u, edge_v], axis=0), ("gx", "pa"), pairs)
    out_u = jnp.logical_or(at_gx == 0, at_gx == gx - 1)
    out_v = at_pa == jnp.where(even, 0, pa - 1)
    far_u = jnp.where(out_u, 0.0, far[:RANK])
    far_v = jnp.where(out_v, 0.0, far[RANK:])
    weights = jnp.transpose(weights, (1, 0, 2))
    gv_mine, gv_other, hi_v, lo_v = gram_v(core, offsets, v, far_v, weights, 1.0 / (v.shape[1] * pa))
    near_u = swap(jnp.where(even, u[:, -LANES:], u[:, :LANES]), "gx", 1)
    left_u = jnp.where(even, far_u, near_u)
    right_u = jnp.where(even, near_u, far_u)
    onehot = (material_index[:, None, :] == jnp.arange(mass_table.shape[1], dtype=jnp.int32)[None, :, None]).astype(F32)
    mass = jnp.sum(mass_table[:, :, None] * onehot, axis=1)
    diffusion = jnp.sum(diffusivity_table[:, :, None] * onehot, axis=1)
    gu_mine, gu_other, hi_u, lo_u = gram_u(core, u, left_u, right_u, mass, diffusion, 1.0 / (u.shape[1] * gx))

    gv = gv_mine + swap(gv_other, "gx", 1)
    bit = 1
    while bit < pa:
        gv = gv + swap(gv, "pa", bit)
        bit *= 2
    gu = gu_mine + swap(gu_other, "gx", 1)
    bit = 2
    while bit < gx:
        gu = gu + swap(gu, "gx", bit)
        bit *= 2
    gv_far = swap(gv, "gx", 1)
    gu_far = swap(gu, "gx", 1)
    sketch_t = make_sketch_t(sketch_seed, WIDE, RANK)
    map_u, map_v, core_next = chain(core, gv, gv_far, gu, gu_far, sketch_t, core_matrix)
    half = next_factor("next_v", map_v, hi_v, lo_v)
    half_far = swap(half, "gx", 1)
    u_next = next_factor("next_u", map_u, hi_u, lo_u)
    v_next = jnp.concatenate([jnp.where(even, half, half_far), jnp.where(even, half_far, half)], axis=1)
    return (u_next, v_next, core_next)


def solution(mesh):
    return jax.shard_map(
        local,
        mesh=mesh,
        in_specs=(
            P(None, "gx"),
            P(None, "pa"),
            P(),
            P(),
            P(None, "gx"),
            P(None, None, "pa"),
            P(),
            P(),
            P(),
        ),
        out_specs=(P(None, "gx"), P(None, "pa"), P()),
        check_vma=False,
    )
```

```python
import functools

import jax
import jax.numpy as jnp
from jax import lax
from jax.experimental import pallas as pl
from jax.experimental.pallas import tpu as pltpu
from jax.sharding import PartitionSpec as P

BAND = 4
LANES = 128
RANK = 64
STENCILS = 4
TAPS = 3
WIDE = 256
F32 = jnp.float32
BF16 = jnp.bfloat16
NT = (((1,), (1,)), ((), ()))
NN = (((1,), (0,)), ((), ()))
VMEM_LIMIT = 14 * 1024 * 1024


def smem():
    return pl.BlockSpec(memory_space=pltpu.SMEM)


def vmem():
    return pl.BlockSpec(memory_space=pltpu.VMEM)


def split(x):
    hi = x.astype(BF16)
    lo = (x - hi.astype(F32)).astype(BF16)
    return hi, lo


def fast_dot(a, b, dims):
    return lax.dot_general(a, b, dims, preferred_element_type=F32)


def full_dot(a, b, dims=NN):
    return lax.dot_general(a, b, dims, precision=lax.Precision.HIGHEST, preferred_element_type=F32)


def lane_iota(shape):
    return lax.broadcasted_iota(jnp.int32, shape, len(shape) - 1)


def shift_left(here, after, by):
    mask = lane_iota(here.shape) < LANES - by
    return jnp.where(mask, pltpu.roll(here, LANES - by, 1), pltpu.roll(after, LANES - by, 1))


def shift_right(before, here, by):
    mask = lane_iota(here.shape) >= by
    return jnp.where(mask, pltpu.roll(here, by, 1), pltpu.roll(before, by, 1))


def finish_gram(hh_ref, hl_ref, pack_ref, scale, core, mine_ref, other_ref):
    for row, col, at in ((0, 0, 0), (128, 0, 128), (128, 128, 256)):
        part = hl_ref[row:row + 128, col:col + 128] + hl_ref[col:col + 128, row:row + 128].T
        pack_ref[at:at + 128, :] = (hh_ref[row:row + 128, col:col + 128] + part) * scale
    half = 192
    mine_ref[...] = pack_ref[pl.ds(pl.multiple_of(core * half, half), half), :]
    other_ref[...] = pack_ref[pl.ds(pl.multiple_of((1 - core) * half, half), half), :]


def add_gram(hi_ref, lo_ref, hh_ref, hl_ref):
    hi = hi_ref[...]
    hh_ref[...] += fast_dot(hi, hi, NT)
    hl_ref[...] += fast_dot(hi, lo_ref[...], NT)


def keep_wide(total, k, near, at, hi_ref, lo_ref, wide_hi, wide_lo):
    rows = slice(k * RANK, (k + 1) * RANK)
    hi, lo = split(total)
    hi_ref[rows, near] = hi
    lo_ref[rows, near] = lo
    wide_hi[rows, at] = hi
    wide_lo[rows, at] = lo


def gram_scratch(part):
    return [pltpu.VMEM((WIDE, part), BF16)] * 4 + [pltpu.VMEM((WIDE, WIDE), F32)] * 2 + [pltpu.VMEM((384, LANES), F32)]


def start_gram(hi_ref, lo_ref, hh_ref, hl_ref):
    hi_ref[...] = jnp.zeros_like(hi_ref)
    lo_ref[...] = jnp.zeros_like(lo_ref)
    hh_ref[...] = jnp.zeros_like(hh_ref)
    hl_ref[...] = jnp.zeros_like(hl_ref)


def shift_all(cells, first, count, moved):
    for i in range(count):
        c = first + i
        lanes = slice(i * LANES, (i + 1) * LANES)
        for by in range(1, BAND + 1):
            moved[BAND + by, :, lanes] = shift_left(cells[c + 1], cells[c + 2], by)
            moved[BAND - by, :, lanes] = shift_right(cells[c], cells[c + 1], by)
        moved[BAND, :, lanes] = cells[c + 1]


def gram_v_kernel(steps, scale, core_ref, off_ref, v_ref, before_ref, after_ref, halo_ref, w_ref,
                  mine_ref, other_ref, wide_hi, wide_lo,
                  moved_a, moved_b, hi_a, lo_a, hi_b, lo_b, hh_ref, hl_ref, pack_ref):
    step = pl.program_id(0)
    core = core_ref[0]
    tile = v_ref.shape[1]
    chunks = tile // LANES
    part = chunks // 2

    @pl.when(step == 0)
    def _():
        start_gram(hi_b, lo_b, hh_ref, hl_ref)

    at_left = jnp.logical_and(step == 0, core == 0)
    at_right = jnp.logical_and(step == steps - 1, core == 1)
    before = jnp.where(at_left, halo_ref[...], before_ref[...])
    after = jnp.where(at_right, halo_ref[...], after_ref[...])
    cells = [before] + [v_ref[:, c * LANES:(c + 1) * LANES] for c in range(chunks)] + [after]
    add_gram(hi_b, lo_b, hh_ref, hl_ref)
    for half, moved, hi_ref, lo_ref in ((0, moved_a, hi_a, lo_a), (1, moved_b, hi_b, lo_b)):
        shift_all(cells, half * part, part, moved)
        for k in range(STENCILS):
            for i in range(part):
                near = slice(i * LANES, (i + 1) * LANES)
                at = slice((half * part + i) * LANES, (half * part + i + 1) * LANES)
                total = w_ref[0, k:k + 1, at] * moved[off_ref[k, 0] + BAND, :, near]
                for t in range(1, TAPS):
                    total = total + w_ref[t, k:k + 1, at] * moved[off_ref[k, t] + BAND, :, near]
                keep_wide(total, k, near, at, hi_ref, lo_ref, wide_hi, wide_lo)
        if half == 0:
            add_gram(hi_a, lo_a, hh_ref, hl_ref)

    @pl.when(step == steps - 1)
    def _():
        add_gram(hi_b, lo_b, hh_ref, hl_ref)
        finish_gram(hh_ref, hl_ref, pack_ref, scale, core, mine_ref, other_ref)


def gram_v(core, offsets, v, halo, weights, scale):
    cells = v.shape[1]
    half = cells // 2
    tile = min(1024, half)
    steps = half // tile
    ratio = tile // LANES
    last = cells // LANES - 1
    spec = pltpu.PrefetchScalarGridSpec(
        num_scalar_prefetch=2,
        grid=(steps,),
        in_specs=[
            pl.BlockSpec((RANK, tile), lambda i, c, o: (0, c[0] * steps + i)),
            pl.BlockSpec((RANK, LANES), lambda i, c, o: (0, jnp.maximum((c[0] * steps + i) * ratio - 1, 0))),
            pl.BlockSpec((RANK, LANES), lambda i, c, o: (0, jnp.minimum((c[0] * steps + i + 1) * ratio, last))),
            pl.BlockSpec((RANK, LANES), lambda i, c, o: (0, 0)),
            pl.BlockSpec((TAPS, STENCILS, tile), lambda i, c, o: (0, 0, c[0] * steps + i)),
        ],
        out_specs=[pl.BlockSpec((192, LANES), lambda i, c, o: (0, 0))] * 2 + [pl.BlockSpec((WIDE, tile), lambda i, c, o: (0, i))] * 2,
        scratch_shapes=[pltpu.VMEM((2 * BAND + 1, RANK, tile // 2), F32)] * 2 + gram_scratch(tile // 2),
    )
    return pl.pallas_call(
        functools.partial(gram_v_kernel, steps, scale),
        grid_spec=spec,
        out_shape=[jax.ShapeDtypeStruct((192, LANES), F32)] * 2 + [jax.ShapeDtypeStruct((WIDE, half), BF16)] * 2,
        compiler_params=pltpu.CompilerParams(vmem_limit_bytes=VMEM_LIMIT),
        name="gram_v",
    )(core, offsets, v, v, v, halo, weights)


def gram_u_kernel(part_at, parts, steps, scale, core_ref, u_ref, before_ref, after_ref, left_ref, right_ref, m_ref, d_ref, *refs):
    if part_at > 0:
        had_mine, had_other, *refs = refs
    mine_ref, other_ref, hi_a, lo_a, hi_b, lo_b, hh_ref, hl_ref, pack_ref = refs
    step = pl.program_id(0)
    chunks = u_ref.shape[1] // LANES
    part = chunks // 2

    @pl.when(step == 0)
    def _():
        start_gram(hi_b, lo_b, hh_ref, hl_ref)

    before, after = before_ref[...], after_ref[...]
    if part_at == 0:
        before = jnp.where(step == 0, left_ref[...], before)
    if part_at == parts - 1:
        after = jnp.where(step == steps - 1, right_ref[...], after)
    cells = [before] + [u_ref[:, c * LANES:(c + 1) * LANES] for c in range(chunks)] + [after]
    add_gram(hi_b, lo_b, hh_ref, hl_ref)
    for half, hi_ref, lo_ref in ((0, hi_a, lo_a), (1, hi_b, lo_b)):
        for i in range(part):
            c = half * part + i
            near = slice(i * LANES, (i + 1) * LANES)
            at = slice(c * LANES, (c + 1) * LANES)
            up = shift_left(cells[c + 1], cells[c + 2], 1)
            down = shift_right(cells[c], cells[c + 1], 1)
            lap = up - 2.0 * cells[c + 1] + down
            for k in range(STENCILS):
                rows = slice(k * RANK, (k + 1) * RANK)
                hi, lo = split(m_ref[k:k + 1, at] * cells[c + 1] + d_ref[k:k + 1, at] * lap)
                hi_ref[rows, near] = hi
                lo_ref[rows, near] = lo
        if half == 0:
            add_gram(hi_a, lo_a, hh_ref, hl_ref)

    @pl.when(step == steps - 1)
    def _():
        add_gram(hi_b, lo_b, hh_ref, hl_ref)
        finish_gram(hh_ref, hl_ref, pack_ref, scale, core_ref[0], mine_ref, other_ref)
        if part_at > 0:
            mine_ref[...] += had_mine[...]
            other_ref[...] += had_other[...]


def gram_u(core, part_at, parts, u, left, right, mass, diffusion, scale, had=()):
    cells = u.shape[1]
    tile = min(1024, cells // parts)
    steps = cells // parts // tile
    first = part_at * steps
    ratio = tile // LANES
    last = cells // LANES - 1
    table = pl.BlockSpec((STENCILS, tile), lambda i, *_: (0, first + i))
    packed = pl.BlockSpec((192, LANES), lambda i, *_: (0, 0))
    spec = pltpu.PrefetchScalarGridSpec(
        num_scalar_prefetch=1,
        grid=(steps,),
        in_specs=[
            pl.BlockSpec((RANK, tile), lambda i, *_: (0, first + i)),
            pl.BlockSpec((RANK, LANES), lambda i, *_: (0, jnp.maximum((first + i) * ratio - 1, 0))),
            pl.BlockSpec((RANK, LANES), lambda i, *_: (0, jnp.minimum((first + i + 1) * ratio, last))),
            pl.BlockSpec((RANK, LANES), lambda i, *_: (0, 0)),
            pl.BlockSpec((RANK, LANES), lambda i, *_: (0, 0)),
            table,
            table,
        ] + [packed] * len(had),
        out_specs=[packed] * 2,
        scratch_shapes=gram_scratch(tile // 2),
    )
    return pl.pallas_call(
        functools.partial(gram_u_kernel, part_at, parts, steps, scale),
        grid_spec=spec,
        out_shape=[jax.ShapeDtypeStruct((192, LANES), F32)] * 2,
        compiler_params=pltpu.CompilerParams(vmem_limit_bytes=VMEM_LIMIT),
        name="gram_u" + str(part_at),
    )(core, u, u, u, left, right, mass, diffusion, *had)


def lower_inverse(square):
    size = RANK
    groups = size // 8
    rows_idx = lax.broadcasted_iota(jnp.int32, (size, size), 0)
    cols_idx = lax.broadcasted_iota(jnp.int32, (size, size), 1)
    unit = jnp.where(rows_idx == cols_idx, 1.0, 0.0).astype(F32)
    both = jnp.concatenate([square, unit], axis=1)
    work = [both[8 * q:8 * q + 8, :] for q in range(groups)]
    shape = (8, 2 * size)
    sub = lax.broadcasted_iota(jnp.int32, shape, 0)
    done = []
    for p in range(groups):
        cols = [[jnp.broadcast_to(work[q][:, 8 * p + j:8 * p + j + 1], shape) for q in range(p, groups)] for j in range(8)]
        rows = [jnp.broadcast_to(work[p][j:j + 1, :], shape) for j in range(8)]
        scaled = []
        kept = None
        for j in range(8):
            pivot = jnp.broadcast_to(cols[j][0][j:j + 1, :], shape)
            inv = 1.0 / pivot
            for k in range(j + 1, 8):
                factor = jnp.broadcast_to(cols[j][0][k:k + 1, :], shape) * inv
                for q in range(groups - p):
                    cols[k][q] = cols[k][q] - cols[j][q] * factor
                rows[k] = rows[k] - rows[j] * factor
            scaled.append(rows[j] * inv)
            unit_row = rows[j] * lax.rsqrt(pivot)
            kept = unit_row if j == 0 else jnp.where(sub == j, unit_row, kept)
        for q in range(p + 1, groups):
            for j in range(8):
                work[q] = work[q] - cols[j][q - p] * scaled[j]
        done.append(kept)
    return jnp.concatenate(done, axis=0)[:, size:]


def unpack(core, mine_ref, other_ref, full_ref):
    first = core == 0
    low = jnp.where(first, mine_ref[...], other_ref[...])
    high = jnp.where(first, other_ref[...], mine_ref[...])
    g10 = jnp.concatenate([low[128:192], high[0:64]], axis=0)
    full_ref[0:128, 0:128] = low[0:128]
    full_ref[128:256, 0:128] = g10
    full_ref[0:128, 128:256] = g10.T
    full_ref[128:256, 128:256] = high[64:192]


def three(x):
    hi, lo = split(x)
    return jnp.concatenate([hi, hi, lo], axis=1)


def put_split(ref, x):
    hi, lo = split(x)
    ref[0:RANK, :] = hi
    ref[RANK:2 * RANK, :] = lo


def chain_kernel(core_ref, gv_mine, gv_other, gu_mine, gu_other, sketch_ref, c_ref, mu_ref, mv_ref, next_ref,
                 gv_ref, gu_ref, panel_ref, block_ref):
    core = core_ref[0]
    unpack(core, gv_mine, gv_other, gv_ref)
    unpack(core, gu_mine, gu_other, gu_ref)
    block_ref[...] = jnp.zeros_like(block_ref)
    for k in range(STENCILS):
        at = slice(k * RANK, (k + 1) * RANK)
        block_ref[at, at] = c_ref[...]
        panel_ref[k] = gv_ref[:, at]
    parts = [None] * STENCILS
    for p in range(STENCILS):
        at = slice(p * RANK, (p + 1) * RANK)
        inverse = lower_inverse(panel_ref[p, at, :])
        below = full_dot(panel_ref[p, p * RANK:, :], inverse, NT)
        for q in range(p + 1, STENCILS):
            head = (q - p) * RANK
            panel_ref[q, q * RANK:, :] -= full_dot(below[head:], below[head:head + RANK], NT)
        for q in range(p, STENCILS):
            head = (q - p) * RANK
            block = below[head:head + RANK]
            if q == p:
                block = jnp.where(
                    lax.broadcasted_iota(jnp.int32, block.shape, 0) >= lane_iota(block.shape), block, 0.0)
            term = full_dot(sketch_ref[p], block, NT)
            parts[q] = term if parts[q] is None else parts[q] + term
    base = jnp.concatenate(parts, axis=1)
    w_t = full_dot(base, block_ref[...], NT)
    k_t = full_dot(w_t, gu_ref[...])
    inverse_y = lower_inverse(full_dot(w_t, k_t, NT))
    x_t = full_dot(inverse_y, full_dot(k_t, block_ref[...]))
    map_u = full_dot(inverse_y, w_t)
    inner = full_dot(x_t, full_dot(x_t, gv_ref[...]), NT)
    inverse_c = lower_inverse(inner)
    map_v = full_dot(inverse_c, x_t)
    lower = full_dot(inner, inverse_c, NT)
    keep = lax.broadcasted_iota(jnp.int32, lower.shape, 0) >= lane_iota(lower.shape)
    next_ref[...] = jnp.where(keep, lower, 0.0)
    for k in range(STENCILS):
        at = slice(k * RANK, (k + 1) * RANK)
        mu_ref[at, :] = three(map_u[:, at])
    put_split(mv_ref, map_v)


def chain(core, gv_mine, gv_other, gu_mine, gu_other, sketch_t, core_matrix):
    return pl.pallas_call(
        chain_kernel,
        in_specs=[smem()] + [vmem()] * 6,
        out_specs=[vmem()] * 3,
        out_shape=[
            jax.ShapeDtypeStruct((WIDE, 3 * RANK), BF16),
            jax.ShapeDtypeStruct((2 * RANK, WIDE), BF16),
            jax.ShapeDtypeStruct((RANK, RANK), F32),
        ],
        scratch_shapes=[
            pltpu.VMEM((WIDE, WIDE), F32),
            pltpu.VMEM((WIDE, WIDE), F32),
            pltpu.VMEM((STENCILS, WIDE, RANK), F32),
            pltpu.VMEM((WIDE, WIDE), F32),
        ],
        compiler_params=pltpu.CompilerParams(vmem_limit_bytes=VMEM_LIMIT),
        name="chain",
    )(core, gv_mine, gv_other, gu_mine, gu_other, sketch_t, core_matrix)


def next_kernel(map_ref, hi_ref, lo_ref, out_ref):
    both = fast_dot(map_ref[...], hi_ref[...], NN)
    out_ref[...] = both[0:RANK] + (both[RANK:2 * RANK] + fast_dot(map_ref[0:RANK, :], lo_ref[...], NN))


def next_factor(name, maps, wide_hi, wide_lo):
    cells = wide_hi.shape[1]
    tile = min(1024, cells)
    return pl.pallas_call(
        next_kernel,
        grid=(cells // tile,),
        in_specs=[
            pl.BlockSpec((2 * RANK, WIDE), lambda i: (0, 0)),
            pl.BlockSpec((WIDE, tile), lambda i: (0, i)),
            pl.BlockSpec((WIDE, tile), lambda i: (0, i)),
        ],
        out_specs=pl.BlockSpec((RANK, tile), lambda i: (0, i)),
        out_shape=jax.ShapeDtypeStruct((RANK, cells), F32),
        compiler_params=pltpu.CompilerParams(vmem_limit_bytes=VMEM_LIMIT),
        name=name,
    )(maps, wide_hi, wide_lo)


def next_u_kernel(steps, u_ref, before_ref, after_ref, left_ref, right_ref, m_ref, d_ref, d_before, d_after, map_ref, out_ref,
                  stack, p_ref):
    step = pl.program_id(0)
    chunks = u_ref.shape[1] // LANES
    before = jnp.where(step == 0, left_ref[...], before_ref[...])
    after = jnp.where(step == steps - 1, right_ref[...], after_ref[...])
    cells = [before] + [u_ref[:, c * LANES:(c + 1) * LANES] for c in range(chunks)] + [after]
    for c in range(chunks + 2):
        at = slice(c * LANES, (c + 1) * LANES)
        hi, lo = split(cells[c])
        stack[0:RANK, at] = hi
        stack[RANK:2 * RANK, at] = lo
        stack[2 * RANK:3 * RANK, at] = hi
    p_ref[...] = fast_dot(map_ref[...], stack[...], NN)
    d = [d_before[...]] + [d_ref[:, c * LANES:(c + 1) * LANES] for c in range(chunks)] + [d_after[...]]

    def weighted(c, table):
        total = None
        for k in range(STENCILS):
            term = table[k:k + 1, :] * p_ref[k * RANK:(k + 1) * RANK, c * LANES:(c + 1) * LANES]
            total = term if total is None else total + term
        return total

    pull = [None] + [weighted(c, shift_right(d[c - 1], d[c], 1)) for c in range(1, chunks + 2)]
    push = [weighted(c, shift_left(d[c], d[c + 1], 1)) for c in range(chunks + 1)]
    for c in range(1, chunks + 1):
        at = slice((c - 1) * LANES, c * LANES)
        near = weighted(c, m_ref[:, at] - 2.0 * d[c])
        out_ref[:, at] = near + (shift_left(pull[c], pull[c + 1], 1) + shift_right(push[c - 1], push[c], 1))


def next_u(u, left, right, mass, diffusion, maps):
    cells = u.shape[1]
    tile = min(1024, cells)
    steps = cells // tile
    ratio = tile // LANES
    last = cells // LANES - 1
    table = pl.BlockSpec((STENCILS, tile), lambda i: (0, i))
    low = lambda i: (0, jnp.maximum(i * ratio - 1, 0))
    high = lambda i: (0, jnp.minimum((i + 1) * ratio, last))
    return pl.pallas_call(
        functools.partial(next_u_kernel, steps),
        grid=(steps,),
        in_specs=[
            pl.BlockSpec((RANK, tile), lambda i: (0, i)),
            pl.BlockSpec((RANK, LANES), low),
            pl.BlockSpec((RANK, LANES), high),
            pl.BlockSpec((RANK, LANES), lambda i: (0, 0)),
            pl.BlockSpec((RANK, LANES), lambda i: (0, 0)),
            table,
            table,
            pl.BlockSpec((STENCILS, LANES), low),
            pl.BlockSpec((STENCILS, LANES), high),
            pl.BlockSpec((WIDE, 3 * RANK), lambda i: (0, 0)),
        ],
        out_specs=pl.BlockSpec((RANK, tile), lambda i: (0, i)),
        out_shape=jax.ShapeDtypeStruct((RANK, cells), F32),
        scratch_shapes=[pltpu.VMEM((3 * RANK, tile + 2 * LANES), BF16), pltpu.VMEM((WIDE, tile + 2 * LANES), F32)],
        compiler_params=pltpu.CompilerParams(vmem_limit_bytes=VMEM_LIMIT),
        name="next_u",
    )(u, u, u, left, right, mass, diffusion, diffusion, diffusion, maps)


def make_sketch_t(sketch_seed, wide, rank):
    shape = (wide // rank, rank, rank)
    rows_idx = lax.broadcasted_iota(jnp.int32, shape, 0) * rank + lax.broadcasted_iota(jnp.int32, shape, 2)
    cols_idx = lax.broadcasted_iota(jnp.int32, shape, 1)
    first = (rows_idx * 131 + cols_idx * 977 + sketch_seed[0]) % 65521
    second = first * 7919 % 65521
    upper = second // 256
    lower = second % 256
    third = (upper * upper * 15 + 512 * upper * lower + lower * lower) % 65521
    fourth = (third * 30011 + rows_idx * 17 + cols_idx) % 65521
    return ((fourth.astype(F32) + 0.5) / 65521.0 - 0.5) * 3.4641


def swap(x, axis, bit):
    return lax.ppermute(x, axis, [(i, i ^ bit) for i in range(lax.axis_size(axis))])


def local(u, v, mass_table, diffusivity_table, material_index, weights, offsets, core_matrix, sketch_seed):
    gx, pa = lax.axis_size("gx"), lax.axis_size("pa")
    at_gx = lax.axis_index("gx")
    core = (at_gx % 2).astype(jnp.int32).reshape(1)
    even = core[0] == 0
    pairs = []
    for g in range(gx):
        for p in range(pa):
            q = p + 1 if g % 2 == 0 else p - 1
            if 0 <= q < pa:
                pairs.append((g * pa + p, g * pa + q))
    edge_v = jnp.where(even, v[:, -LANES:], v[:, :LANES])
    halo_v = lax.ppermute(edge_v, ("gx", "pa"), pairs)
    onehot = (material_index[:, None, :] == jnp.arange(mass_table.shape[1], dtype=jnp.int32)[None, :, None]).astype(F32)
    mass = jnp.sum(mass_table[:, :, None] * onehot, axis=1)
    diffusion = jnp.sum(diffusivity_table[:, :, None] * onehot, axis=1)
    sketch_t = make_sketch_t(sketch_seed, WIDE, RANK)
    v_in, mass, diffusion, sketch_t = lax.optimization_barrier((v, mass, diffusion, sketch_t))
    weights = jnp.transpose(weights, (1, 0, 2))
    gv_mine, gv_other, hi_v, lo_v = gram_v(core, offsets, v_in, halo_v, weights, 1.0 / (v.shape[1] * pa))
    gv = gv_mine + swap(gv_other, "gx", 1)

    u_pairs = [(i, i - 1 if i % 2 == 0 else i + 1) for i in range(gx)]
    far_u = lax.ppermute(jnp.where(even, u[:, :LANES], u[:, -LANES:]), "gx", [(i, j) for i, j in u_pairs if 0 <= j < gx])
    near_u = swap(jnp.where(even, u[:, -LANES:], u[:, :LANES]), "gx", 1)
    left_u = jnp.where(even, far_u, near_u)
    right_u = jnp.where(even, near_u, far_u)
    u_scale = 1.0 / (u.shape[1] * gx)
    had = gram_u(core, 0, 2, u, left_u, right_u, mass, diffusion, u_scale)
    gu_mine, gu_other = gram_u(core, 1, 2, u, left_u, right_u, mass, diffusion, u_scale, had)

    bit = 1
    while bit < pa:
        gv = gv + swap(gv, "pa", bit)
        bit *= 2
    gu = gu_mine + swap(gu_other, "gx", 1)
    bit = 2
    while bit < gx:
        gu = gu + swap(gu, "gx", bit)
        bit *= 2
    gv_far = swap(gv, "gx", 1)
    gu_far = swap(gu, "gx", 1)
    map_u, map_v, core_next = chain(core, gv, gv_far, gu, gu_far, sketch_t, core_matrix)
    half = next_factor("next_v", map_v, hi_v, lo_v)
    half_far = swap(half, "gx", 1)
    u_next = next_u(u, left_u, right_u, mass, diffusion, map_u)
    v_next = jnp.concatenate([jnp.where(even, half, half_far), jnp.where(even, half_far, half)], axis=1)
    return (u_next, v_next, core_next)


def solution(mesh):
    return jax.shard_map(
        local,
        mesh=mesh,
        in_specs=(
            P(None, "gx"),
            P(None, "pa"),
            P(),
            P(),
            P(None, "gx"),
            P(None, None, "pa"),
            P(),
            P(),
            P(),
        ),
        out_specs=(P(None, "gx"), P(None, "pa"), P()),
        check_vma=False,
    )
```

```python
import functools

import jax
import jax.numpy as jnp
from jax import lax
from jax.experimental import pallas as pl
from jax.experimental.pallas import tpu as pltpu
from jax.sharding import PartitionSpec as P


BAND = 4
LANES = 128
RANK = 64
STENCILS = 4
TAPS = 3
WIDE = 256
F32 = jnp.float32
BF16 = jnp.bfloat16
NT = (((1,), (1,)), ((), ()))
NN = (((1,), (0,)), ((), ()))
VMEM_LIMIT = 14 * 1024 * 1024


def smem():
    return pl.BlockSpec(memory_space=pltpu.SMEM)


def vmem():
    return pl.BlockSpec(memory_space=pltpu.VMEM)


def split(x):
    hi = x.astype(BF16)
    lo = (x - hi.astype(F32)).astype(BF16)
    return hi, lo


def fast_dot(a, b, dims):
    return lax.dot_general(a, b, dims, preferred_element_type=F32)


def full_dot(a, b, dims=NN):
    return lax.dot_general(a, b, dims, precision=lax.Precision.HIGHEST, preferred_element_type=F32)


def split_dot(a, b, dims=NN):
    a_hi, a_lo = split(a)
    b_hi, b_lo = split(b)
    small = fast_dot(a_hi, b_lo, dims) + fast_dot(a_lo, b_hi, dims)
    return fast_dot(a_hi, b_hi, dims) + small


def lane_iota(shape):
    return lax.broadcasted_iota(jnp.int32, shape, len(shape) - 1)


def shift_left(here, after, by):
    mask = lane_iota(here.shape) < LANES - by
    return jnp.where(mask, pltpu.roll(here, LANES - by, 1), pltpu.roll(after, LANES - by, 1))


def shift_right(before, here, by):
    mask = lane_iota(here.shape) >= by
    return jnp.where(mask, pltpu.roll(here, by, 1), pltpu.roll(before, by, 1))


def finish_gram(hh_ref, hl_ref, pack_ref, scale, core, mine_ref, other_ref):
    for row, col, at in ((0, 0, 0), (128, 0, 128), (128, 128, 256)):
        part = hl_ref[row:row + 128, col:col + 128] + hl_ref[col:col + 128, row:row + 128].T
        pack_ref[at:at + 128, :] = (hh_ref[row:row + 128, col:col + 128] + part) * scale
    half = 192
    mine_ref[...] = pack_ref[pl.ds(pl.multiple_of(core * half, half), half), :]
    other_ref[...] = pack_ref[pl.ds(pl.multiple_of((1 - core) * half, half), half), :]


def add_gram(hi_ref, lo_ref, hh_ref, hl_ref):
    hi = hi_ref[...]
    hh_ref[...] += fast_dot(hi, hi, NT)
    hl_ref[...] += fast_dot(hi, lo_ref[...], NT)


def keep_wide(total, k, near, at, hi_ref, lo_ref, wide_hi, wide_lo):
    rows = slice(k * RANK, (k + 1) * RANK)
    hi, lo = split(total)
    hi_ref[rows, near] = hi
    lo_ref[rows, near] = lo
    wide_hi[rows, at] = hi
    wide_lo[rows, at] = lo


def gram_scratch(part):
    return [pltpu.VMEM((WIDE, part), BF16)] * 4 + [pltpu.VMEM((WIDE, WIDE), F32)] * 2 + [pltpu.VMEM((384, LANES), F32)]


def start_gram(hi_ref, lo_ref, hh_ref, hl_ref):
    hi_ref[...] = jnp.zeros_like(hi_ref)
    lo_ref[...] = jnp.zeros_like(lo_ref)
    hh_ref[...] = jnp.zeros_like(hh_ref)
    hl_ref[...] = jnp.zeros_like(hl_ref)


def shift_all(cells, first, count, moved):
    for i in range(count):
        c = first + i
        lanes = slice(i * LANES, (i + 1) * LANES)
        for by in range(1, BAND + 1):
            moved[BAND + by, :, lanes] = shift_left(cells[c + 1], cells[c + 2], by)
            moved[BAND - by, :, lanes] = shift_right(cells[c], cells[c + 1], by)
        moved[BAND, :, lanes] = cells[c + 1]


def gram_v_kernel(steps, scale, core_ref, off_ref, v_ref, before_ref, after_ref, halo_ref, w_ref,
                  mine_ref, other_ref, wide_hi, wide_lo,
                  moved_a, moved_b, hi_a, lo_a, hi_b, lo_b, hh_ref, hl_ref, pack_ref):
    step = pl.program_id(0)
    core = core_ref[0]
    tile = v_ref.shape[1]
    chunks = tile // LANES
    part = chunks // 2

    @pl.when(step == 0)
    def _():
        start_gram(hi_b, lo_b, hh_ref, hl_ref)

    at_left = jnp.logical_and(step == 0, core == 0)
    at_right = jnp.logical_and(step == steps - 1, core == 1)
    before = jnp.where(at_left, halo_ref[...], before_ref[...])
    after = jnp.where(at_right, halo_ref[...], after_ref[...])
    cells = [before] + [v_ref[:, c * LANES:(c + 1) * LANES] for c in range(chunks)] + [after]
    add_gram(hi_b, lo_b, hh_ref, hl_ref)
    for half, moved, hi_ref, lo_ref in ((0, moved_a, hi_a, lo_a), (1, moved_b, hi_b, lo_b)):
        shift_all(cells, half * part, part, moved)
        for k in range(STENCILS):
            for i in range(part):
                near = slice(i * LANES, (i + 1) * LANES)
                at = slice((half * part + i) * LANES, (half * part + i + 1) * LANES)
                total = w_ref[0, k:k + 1, at] * moved[off_ref[k, 0] + BAND, :, near]
                for t in range(1, TAPS):
                    total = total + w_ref[t, k:k + 1, at] * moved[off_ref[k, t] + BAND, :, near]
                keep_wide(total, k, near, at, hi_ref, lo_ref, wide_hi, wide_lo)
        if half == 0:
            add_gram(hi_a, lo_a, hh_ref, hl_ref)

    @pl.when(step == steps - 1)
    def _():
        add_gram(hi_b, lo_b, hh_ref, hl_ref)
        finish_gram(hh_ref, hl_ref, pack_ref, scale, core, mine_ref, other_ref)


def gram_v(core, offsets, v, halo, weights, scale):
    cells = v.shape[1]
    half = cells // 2
    tile = min(1024, half)
    steps = half // tile
    ratio = tile // LANES
    last = cells // LANES - 1
    spec = pltpu.PrefetchScalarGridSpec(
        num_scalar_prefetch=2,
        grid=(steps,),
        in_specs=[
            pl.BlockSpec((RANK, tile), lambda i, c, o: (0, c[0] * steps + i)),
            pl.BlockSpec((RANK, LANES), lambda i, c, o: (0, jnp.maximum((c[0] * steps + i) * ratio - 1, 0))),
            pl.BlockSpec((RANK, LANES), lambda i, c, o: (0, jnp.minimum((c[0] * steps + i + 1) * ratio, last))),
            pl.BlockSpec((RANK, LANES), lambda i, c, o: (0, 0)),
            pl.BlockSpec((TAPS, STENCILS, tile), lambda i, c, o: (0, 0, c[0] * steps + i)),
        ],
        out_specs=[pl.BlockSpec((192, LANES), lambda i, c, o: (0, 0))] * 2 + [pl.BlockSpec((WIDE, tile), lambda i, c, o: (0, i))] * 2,
        scratch_shapes=[pltpu.VMEM((2 * BAND + 1, RANK, tile // 2), F32)] * 2 + gram_scratch(tile // 2),
    )
    return pl.pallas_call(
        functools.partial(gram_v_kernel, steps, scale),
        grid_spec=spec,
        out_shape=[jax.ShapeDtypeStruct((192, LANES), F32)] * 2 + [jax.ShapeDtypeStruct((WIDE, half), BF16)] * 2,
        compiler_params=pltpu.CompilerParams(vmem_limit_bytes=VMEM_LIMIT),
        name="gram_v",
    )(core, offsets, v, v, v, halo, weights)


def gram_u_kernel(part_at, parts, steps, scale, core_ref, u_ref, before_ref, after_ref, left_ref, right_ref, m_ref, d_ref, *refs):
    if part_at > 0:
        had_mine, had_other, *refs = refs
    mine_ref, other_ref, hi_a, lo_a, hi_b, lo_b, hh_ref, hl_ref, pack_ref = refs
    step = pl.program_id(0)
    chunks = u_ref.shape[1] // LANES
    part = chunks // 2

    @pl.when(step == 0)
    def _():
        start_gram(hi_b, lo_b, hh_ref, hl_ref)

    before, after = before_ref[...], after_ref[...]
    if part_at == 0:
        before = jnp.where(step == 0, left_ref[...], before)
    if part_at == parts - 1:
        after = jnp.where(step == steps - 1, right_ref[...], after)
    cells = [before] + [u_ref[:, c * LANES:(c + 1) * LANES] for c in range(chunks)] + [after]
    add_gram(hi_b, lo_b, hh_ref, hl_ref)
    for half, hi_ref, lo_ref in ((0, hi_a, lo_a), (1, hi_b, lo_b)):
        for i in range(part):
            c = half * part + i
            near = slice(i * LANES, (i + 1) * LANES)
            at = slice(c * LANES, (c + 1) * LANES)
            up = shift_left(cells[c + 1], cells[c + 2], 1)
            down = shift_right(cells[c], cells[c + 1], 1)
            lap = up - 2.0 * cells[c + 1] + down
            for k in range(STENCILS):
                rows = slice(k * RANK, (k + 1) * RANK)
                hi, lo = split(m_ref[k:k + 1, at] * cells[c + 1] + d_ref[k:k + 1, at] * lap)
                hi_ref[rows, near] = hi
                lo_ref[rows, near] = lo
        if half == 0:
            add_gram(hi_a, lo_a, hh_ref, hl_ref)

    @pl.when(step == steps - 1)
    def _():
        add_gram(hi_b, lo_b, hh_ref, hl_ref)
        finish_gram(hh_ref, hl_ref, pack_ref, scale, core_ref[0], mine_ref, other_ref)
        if part_at > 0:
            mine_ref[...] += had_mine[...]
            other_ref[...] += had_other[...]


def gram_u(core, part_at, parts, u, left, right, mass, diffusion, scale, had=()):
    cells = u.shape[1]
    tile = min(1024, cells // parts)
    steps = cells // parts // tile
    first = part_at * steps
    ratio = tile // LANES
    last = cells // LANES - 1
    table = pl.BlockSpec((STENCILS, tile), lambda i, *_: (0, first + i))
    packed = pl.BlockSpec((192, LANES), lambda i, *_: (0, 0))
    spec = pltpu.PrefetchScalarGridSpec(
        num_scalar_prefetch=1,
        grid=(steps,),
        in_specs=[
            pl.BlockSpec((RANK, tile), lambda i, *_: (0, first + i)),
            pl.BlockSpec((RANK, LANES), lambda i, *_: (0, jnp.maximum((first + i) * ratio - 1, 0))),
            pl.BlockSpec((RANK, LANES), lambda i, *_: (0, jnp.minimum((first + i + 1) * ratio, last))),
            pl.BlockSpec((RANK, LANES), lambda i, *_: (0, 0)),
            pl.BlockSpec((RANK, LANES), lambda i, *_: (0, 0)),
            table,
            table,
        ] + [packed] * len(had),
        out_specs=[packed] * 2,
        scratch_shapes=gram_scratch(tile // 2),
    )
    return pl.pallas_call(
        functools.partial(gram_u_kernel, part_at, parts, steps, scale),
        grid_spec=spec,
        out_shape=[jax.ShapeDtypeStruct((192, LANES), F32)] * 2,
        compiler_params=pltpu.CompilerParams(vmem_limit_bytes=VMEM_LIMIT),
    )(core, u, u, u, left, right, mass, diffusion, *had)


def lower_inverse(square, zero):
    size = RANK
    groups = size // 8
    rows_idx = lax.broadcasted_iota(jnp.int32, (size, size), 0)
    unit = jnp.where(rows_idx == lane_iota((size, size)), 1.0, 0.0).astype(F32)
    both = jnp.concatenate([square, unit], axis=1)
    work = [both[8 * q:8 * q + 8, :] for q in range(groups)]
    shape = (8, 2 * size)
    sub = lax.broadcasted_iota(jnp.int32, shape, 0)

    def lane(x, at):
        return jnp.broadcast_to(x[:, at:at + 1], shape)

    def row(x, at):
        return jnp.broadcast_to(x[at:at + 1, :], shape)

    done = []
    for p in range(groups):
        cols = [lane(work[p], 8 * p + j) + zero for j in range(8)]
        rows = [row(work[p], j) for j in range(8)]
        kept = None
        invs = []
        for j in range(8):
            pivot = row(cols[j], j)
            inv = 1.0 / pivot
            unit_row = rows[j] * lax.rsqrt(pivot)
            kept = unit_row if j == 0 else jnp.where(sub == j, unit_row, kept)
            last = p == groups - 1
            above = cols[j] if last else jnp.where(sub == j, 0.0, cols[j])
            for k in range(j + 1, 8):
                cols[k] = cols[k] - above * (row(cols[j], k) * inv)
            scaled = rows[j] * inv
            for k in range(j + 1 if last else 0, 8):
                if k != j:
                    rows[k] = rows[k] - scaled * row(cols[j], k)
            invs.append(inv)
        if p < groups - 1:
            rows = [r * inv for r, inv in zip(rows, invs)]
        for q in range(p + 1, groups):
            terms = [lane(work[q], 8 * p + j) * rows[j] for j in range(8)]
            while len(terms) > 1:
                terms = [terms[i] + terms[i + 1] for i in range(0, len(terms), 2)]
            work[q] = work[q] - terms[0]
        done.append(kept)
    return jnp.concatenate(done, axis=0)[:, size:]


def unpack(core, mine_ref, other_ref, full_ref):
    first = core == 0
    low = jnp.where(first, mine_ref[...], other_ref[...])
    high = jnp.where(first, other_ref[...], mine_ref[...])
    g10 = jnp.concatenate([low[128:192], high[0:64]], axis=0)
    full_ref[0:128, 0:128] = low[0:128]
    full_ref[128:256, 0:128] = g10
    full_ref[0:128, 128:256] = g10.T
    full_ref[128:256, 128:256] = high[64:192]


def three(x):
    hi, lo = split(x)
    return jnp.concatenate([hi, hi, lo], axis=1)


def put_split(ref, x):
    hi, lo = split(x)
    ref[0:RANK, :] = hi
    ref[RANK:2 * RANK, :] = lo


def chain_kernel(core_ref, gv_mine, gv_other, gu_mine, gu_other, sketch_ref, c_ref, mu_ref, mv_ref, next_ref,
                 gv_ref, gu_ref, panel_ref):
    core = core_ref[0]
    zero = jnp.where(core > 1, 1.0, 0.0).astype(F32)
    unpack(core, gv_mine, gv_other, gv_ref)
    unpack(core, gu_mine, gu_other, gu_ref)
    blocks = [slice(k * RANK, (k + 1) * RANK) for k in range(STENCILS)]
    for k in range(STENCILS):
        panel_ref[k] = gv_ref[:, blocks[k]]
    c = c_ref[...]
    low = lax.broadcasted_iota(jnp.int32, (RANK, RANK), 0) >= lane_iota((RANK, RANK))
    parts = [None] * STENCILS
    w = []
    k_t = None
    for p in range(STENCILS):
        inverse = lower_inverse(panel_ref[p, blocks[p], :], zero)
        below = full_dot(panel_ref[p, p * RANK:, :], inverse, NT)
        for q in range(p + 1, STENCILS):
            head = (q - p) * RANK
            panel_ref[q, q * RANK:, :] -= full_dot(below[head:], below[head:head + RANK], NT)
        for q in range(p, STENCILS):
            head = (q - p) * RANK
            block = below[head:head + RANK]
            if q == p:
                block = jnp.where(low, block, 0.0)
            term = split_dot(sketch_ref[p], block, NT)
            parts[q] = term if parts[q] is None else parts[q] + term
        w.append(split_dot(parts[p], c, NT))
        term = full_dot(w[p], gu_ref[blocks[p], :])
        k_t = term if k_t is None else k_t + term
    w_t = jnp.concatenate(w, axis=1)
    inverse_y = lower_inverse(full_dot(w_t, k_t, NT), zero)
    back = jnp.concatenate([split_dot(k_t[:, at], c) for at in blocks], axis=1)
    back_gram = full_dot(back, gv_ref[...])
    x_t = full_dot(inverse_y, back)
    inner = full_dot(x_t, full_dot(inverse_y, back_gram), NT)
    inverse_c = lower_inverse(inner, zero)
    map_u = split_dot(inverse_y, w_t)
    for k in range(STENCILS):
        mu_ref[blocks[k], :] = three(map_u[:, blocks[k]])
    put_split(mv_ref, split_dot(inverse_c, x_t))
    next_ref[...] = jnp.where(low, full_dot(inner, inverse_c, NT), 0.0)


def chain(core, gv_mine, gv_other, gu_mine, gu_other, sketch_t, core_matrix):
    return pl.pallas_call(
        chain_kernel,
        in_specs=[smem()] + [vmem()] * 6,
        out_specs=[vmem()] * 3,
        out_shape=[
            jax.ShapeDtypeStruct((WIDE, 3 * RANK), BF16),
            jax.ShapeDtypeStruct((2 * RANK, WIDE), BF16),
            jax.ShapeDtypeStruct((RANK, RANK), F32),
        ],
        scratch_shapes=[
            pltpu.VMEM((WIDE, WIDE), F32),
            pltpu.VMEM((WIDE, WIDE), F32),
            pltpu.VMEM((STENCILS, WIDE, RANK), F32),
        ],
        compiler_params=pltpu.CompilerParams(vmem_limit_bytes=VMEM_LIMIT),
        name="chain",
    )(core, gv_mine, gv_other, gu_mine, gu_other, sketch_t, core_matrix)


def next_kernel(map_ref, hi_ref, lo_ref, out_ref):
    both = fast_dot(map_ref[...], hi_ref[...], NN)
    out_ref[...] = both[0:RANK] + (both[RANK:2 * RANK] + fast_dot(map_ref[0:RANK, :], lo_ref[...], NN))


def next_factor(maps, wide_hi, wide_lo):
    cells = wide_hi.shape[1]
    tile = min(1024, cells)
    return pl.pallas_call(
        next_kernel,
        grid=(cells // tile,),
        in_specs=[
            pl.BlockSpec((2 * RANK, WIDE), lambda i: (0, 0)),
            pl.BlockSpec((WIDE, tile), lambda i: (0, i)),
            pl.BlockSpec((WIDE, tile), lambda i: (0, i)),
        ],
        out_specs=pl.BlockSpec((RANK, tile), lambda i: (0, i)),
        out_shape=jax.ShapeDtypeStruct((RANK, cells), F32),
        compiler_params=pltpu.CompilerParams(vmem_limit_bytes=VMEM_LIMIT),
    )(maps, wide_hi, wide_lo)


def next_u_kernel(steps, u_ref, before_ref, after_ref, left_ref, right_ref, m_ref, d_ref, d_before, d_after, map_ref, out_ref,
                  stack, p_ref):
    step = pl.program_id(0)
    chunks = u_ref.shape[1] // LANES
    before = jnp.where(step == 0, left_ref[...], before_ref[...])
    after = jnp.where(step == steps - 1, right_ref[...], after_ref[...])
    cells = [before] + [u_ref[:, c * LANES:(c + 1) * LANES] for c in range(chunks)] + [after]
    for c in range(chunks + 2):
        at = slice(c * LANES, (c + 1) * LANES)
        hi, lo = split(cells[c])
        stack[0:RANK, at] = hi
        stack[RANK:2 * RANK, at] = lo
        stack[2 * RANK:3 * RANK, at] = hi
    p_ref[...] = fast_dot(map_ref[...], stack[...], NN)
    d = [d_before[...]] + [d_ref[:, c * LANES:(c + 1) * LANES] for c in range(chunks)] + [d_after[...]]

    def weighted(c, table):
        total = None
        for k in range(STENCILS):
            term = table[k:k + 1, :] * p_ref[k * RANK:(k + 1) * RANK, c * LANES:(c + 1) * LANES]
            total = term if total is None else total + term
        return total

    pull = [None] + [weighted(c, shift_right(d[c - 1], d[c], 1)) for c in range(1, chunks + 2)]
    push = [weighted(c, shift_left(d[c], d[c + 1], 1)) for c in range(chunks + 1)]
    for c in range(1, chunks + 1):
        at = slice((c - 1) * LANES, c * LANES)
        near = weighted(c, m_ref[:, at] - 2.0 * d[c])
        out_ref[:, at] = near + (shift_left(pull[c], pull[c + 1], 1) + shift_right(push[c - 1], push[c], 1))


def next_u(u, left, right, mass, diffusion, maps):
    cells = u.shape[1]
    tile = min(1024, cells)
    steps = cells // tile
    ratio = tile // LANES
    last = cells // LANES - 1
    table = pl.BlockSpec((STENCILS, tile), lambda i: (0, i))
    low = lambda i: (0, jnp.maximum(i * ratio - 1, 0))
    high = lambda i: (0, jnp.minimum((i + 1) * ratio, last))
    return pl.pallas_call(
        functools.partial(next_u_kernel, steps),
        grid=(steps,),
        in_specs=[
            pl.BlockSpec((RANK, tile), lambda i: (0, i)),
            pl.BlockSpec((RANK, LANES), low),
            pl.BlockSpec((RANK, LANES), high),
            pl.BlockSpec((RANK, LANES), lambda i: (0, 0)),
            pl.BlockSpec((RANK, LANES), lambda i: (0, 0)),
            table,
            table,
            pl.BlockSpec((STENCILS, LANES), low),
            pl.BlockSpec((STENCILS, LANES), high),
            pl.BlockSpec((WIDE, 3 * RANK), lambda i: (0, 0)),
        ],
        out_specs=pl.BlockSpec((RANK, tile), lambda i: (0, i)),
        out_shape=jax.ShapeDtypeStruct((RANK, cells), F32),
        scratch_shapes=[pltpu.VMEM((3 * RANK, tile + 2 * LANES), BF16), pltpu.VMEM((WIDE, tile + 2 * LANES), F32)],
        compiler_params=pltpu.CompilerParams(vmem_limit_bytes=VMEM_LIMIT),
        name="next_u",
    )(u, u, u, left, right, mass, diffusion, diffusion, diffusion, maps)


def make_sketch_t(sketch_seed, wide, rank):
    shape = (wide // rank, rank, rank)
    rows_idx = lax.broadcasted_iota(jnp.int32, shape, 0) * rank + lax.broadcasted_iota(jnp.int32, shape, 2)
    cols_idx = lax.broadcasted_iota(jnp.int32, shape, 1)
    first = (rows_idx * 131 + cols_idx * 977 + sketch_seed[0]) % 65521
    second = first * 7919 % 65521
    upper = second // 256
    lower = second % 256
    third = (upper * upper * 15 + 512 * upper * lower + lower * lower) % 65521
    fourth = (third * 30011 + rows_idx * 17 + cols_idx) % 65521
    return ((fourth.astype(F32) + 0.5) / 65521.0 - 0.5) * 3.4641


def swap(x, axis, bit):
    return lax.ppermute(x, axis, [(i, i ^ bit) for i in range(lax.axis_size(axis))])


def four_way(x, axis, bit):
    near, far, both = (swap(x, axis, b) for b in (bit, 2 * bit, 3 * bit))
    return (x + near) + (far + both)


def body(u, v, mass_table, diffusivity_table, material_index, weights, offsets, core_matrix, sketch_seed):
    gx, pa = lax.axis_size("gx"), lax.axis_size("pa")
    at_gx = lax.axis_index("gx")
    core = (at_gx % 2).astype(jnp.int32).reshape(1)
    even = core[0] == 0
    pairs = []
    for g in range(gx):
        for p in range(pa):
            q = p + 1 if g % 2 == 0 else p - 1
            if 0 <= q < pa:
                pairs.append((g * pa + p, g * pa + q))
    edge_v = jnp.where(even, v[:, -LANES:], v[:, :LANES])
    halo_v = lax.ppermute(edge_v, ("gx", "pa"), pairs)
    onehot = (material_index[:, None, :] == jnp.arange(mass_table.shape[1], dtype=jnp.int32)[None, :, None]).astype(F32)
    mass = jnp.sum(mass_table[:, :, None] * onehot, axis=1)
    diffusion = jnp.sum(diffusivity_table[:, :, None] * onehot, axis=1)
    near_u = swap(jnp.where(even, u[:, -LANES:], u[:, :LANES]), "gx", 1)
    u_pairs = [(i, i - 1 if i % 2 == 0 else i + 1) for i in range(gx)]
    far_u = lax.ppermute(jnp.where(even, u[:, :LANES], u[:, -LANES:]), "gx", [(i, j) for i, j in u_pairs if 0 <= j < gx])
    core_v, mass, diffusion = lax.optimization_barrier((core, mass, diffusion))
    weights = pltpu.with_memory_space_constraint(jnp.transpose(weights, (1, 0, 2)), pltpu.HBM)
    v_in = pltpu.with_memory_space_constraint(v, pltpu.HBM)
    gv_mine, gv_other, hi_v, lo_v = gram_v(core_v, pltpu.with_memory_space_constraint(offsets, pltpu.HBM), v_in, halo_v, weights, 1.0 / (v.shape[1] * pa))
    gv = gv_mine + swap(gv_other, "gx", 1)

    left_u = jnp.where(even, far_u, near_u)
    right_u = jnp.where(even, near_u, far_u)
    u_scale = 1.0 / (u.shape[1] * gx)
    had = gram_u(core, 0, 2, u, left_u, right_u, mass, diffusion, u_scale)
    gu_mine, gu_other = gram_u(core, 1, 2, u, left_u, right_u, mass, diffusion, u_scale, had)
    sketch_t = make_sketch_t(sketch_seed, WIDE, RANK)

    bit = 1
    while bit * 4 < pa:
        gv = gv + swap(gv, "pa", bit)
        bit *= 2
    gu = four_way(gu_mine + swap(gu_other, "gx", 1), "gx", 2)
    gv = four_way(gv, "pa", bit)
    gv_far = swap(gv, "gx", 1)
    gu_far = swap(gu, "gx", 1)
    map_u, map_v, core_next = chain(core, gv, gv_far, gu, gu_far, sketch_t, core_matrix)
    half = next_factor(map_v, hi_v, lo_v)
    half_far = swap(half, "gx", 1)
    u_next = next_u(u, left_u, right_u, mass, diffusion, map_u)
    v_next = jnp.concatenate([jnp.where(even, half, half_far), jnp.where(even, half_far, half)], axis=1)
    return (u_next, v_next, core_next)


def solution(mesh):
    return jax.shard_map(
        body,
        mesh=mesh,
        in_specs=(
            P(None, "gx"),
            P(None, "pa"),
            P(),
            P(),
            P(None, "gx"),
            P(None, None, "pa"),
            P(),
            P(),
            P(),
        ),
        out_specs=(P(None, "gx"), P(None, "pa"), P()),
        check_vma=False,
    )
```

```python
import functools

import jax
import jax.numpy as jnp
from jax import lax
from jax.experimental import pallas as pl
from jax.experimental.pallas import tpu as pltpu
from jax.sharding import PartitionSpec as P


BAND = 4
LANES = 128
RANK = 64
STENCILS = 4
TAPS = 3
WIDE = 256
F32 = jnp.float32
BF16 = jnp.bfloat16
NT = (((1,), (1,)), ((), ()))
NN = (((1,), (0,)), ((), ()))
VMEM_LIMIT = 16 * 1024 * 1024


def smem():
    return pl.BlockSpec(memory_space=pltpu.SMEM)


def vmem():
    return pl.BlockSpec(memory_space=pltpu.VMEM)


def split(x):
    hi = x.astype(BF16)
    lo = (x - hi.astype(F32)).astype(BF16)
    return hi, lo


def fast_dot(a, b, dims):
    return lax.dot_general(a, b, dims, preferred_element_type=F32)


def full_dot(a, b, dims=NN):
    return lax.dot_general(a, b, dims, precision=lax.Precision.HIGHEST, preferred_element_type=F32)


def split_dot(a, b, dims=NN):
    a_hi, a_lo = split(a)
    b_hi, b_lo = split(b)
    small = fast_dot(a_hi, b_lo, dims) + fast_dot(a_lo, b_hi, dims)
    return fast_dot(a_hi, b_hi, dims) + small


def lane_iota(shape):
    return lax.broadcasted_iota(jnp.int32, shape, len(shape) - 1)


def shift_left(here, after, by):
    mask = lane_iota(here.shape) < LANES - by
    return jnp.where(mask, pltpu.roll(here, LANES - by, 1), pltpu.roll(after, LANES - by, 1))


def shift_right(before, here, by):
    mask = lane_iota(here.shape) >= by
    return jnp.where(mask, pltpu.roll(here, by, 1), pltpu.roll(before, by, 1))


def finish_gram(hh_ref, hl_ref, pack_ref, scale, core, mine_ref, other_ref):
    for row, col, at in ((0, 0, 0), (128, 0, 128), (128, 128, 256)):
        part = hl_ref[row:row + 128, col:col + 128] + hl_ref[col:col + 128, row:row + 128].T
        pack_ref[at:at + 128, :] = (hh_ref[row:row + 128, col:col + 128] + part) * scale
    half = 192
    mine_ref[...] = pack_ref[pl.ds(pl.multiple_of(core * half, half), half), :]
    other_ref[...] = pack_ref[pl.ds(pl.multiple_of((1 - core) * half, half), half), :]


def add_gram(hi_ref, lo_ref, hh_ref, hl_ref):
    hi = hi_ref[...]
    hh_ref[...] += fast_dot(hi, hi, NT)
    hl_ref[...] += fast_dot(hi, lo_ref[...], NT)


def keep_wide(total, k, near, at, hi_ref, lo_ref, wide_hi, wide_lo):
    rows = slice(k * RANK, (k + 1) * RANK)
    hi, lo = split(total)
    hi_ref[rows, near] = hi
    lo_ref[rows, near] = lo
    wide_hi[rows, at] = hi
    wide_lo[rows, at] = lo


def gram_scratch(part):
    return [pltpu.VMEM((WIDE, part), BF16)] * 4 + [pltpu.VMEM((WIDE, WIDE), F32)] * 2 + [pltpu.VMEM((384, LANES), F32)]


def start_gram(hi_ref, lo_ref, hh_ref, hl_ref):
    hi_ref[...] = jnp.zeros_like(hi_ref)
    lo_ref[...] = jnp.zeros_like(lo_ref)
    hh_ref[...] = jnp.zeros_like(hh_ref)
    hl_ref[...] = jnp.zeros_like(hl_ref)


def shift_all(cells, first, count, moved):
    for i in range(count):
        c = first + i
        lanes = slice(i * LANES, (i + 1) * LANES)
        for by in range(1, BAND + 1):
            moved[BAND + by, :, lanes] = shift_left(cells[c + 1], cells[c + 2], by)
            moved[BAND - by, :, lanes] = shift_right(cells[c], cells[c + 1], by)
        moved[BAND, :, lanes] = cells[c + 1]


def gram_v_kernel(steps, scale, core_ref, off_ref, v_ref, before_ref, after_ref, halo_ref, w_ref,
                  mine_ref, other_ref, wide_hi, wide_lo,
                  moved_a, moved_b, hi_a, lo_a, hi_b, lo_b, hh_ref, hl_ref, pack_ref):
    step = pl.program_id(0)
    core = core_ref[0]
    tile = v_ref.shape[1]
    chunks = tile // LANES
    part = chunks // 2

    @pl.when(step == 0)
    def _():
        start_gram(hi_b, lo_b, hh_ref, hl_ref)

    at_left = jnp.logical_and(step == 0, core == 0)
    at_right = jnp.logical_and(step == steps - 1, core == 1)
    before = jnp.where(at_left, halo_ref[...], before_ref[...])
    after = jnp.where(at_right, halo_ref[...], after_ref[...])
    cells = [before] + [v_ref[:, c * LANES:(c + 1) * LANES] for c in range(chunks)] + [after]
    add_gram(hi_b, lo_b, hh_ref, hl_ref)
    for half, moved, hi_ref, lo_ref in ((0, moved_a, hi_a, lo_a), (1, moved_b, hi_b, lo_b)):
        shift_all(cells, half * part, part, moved)
        for k in range(STENCILS):
            for i in range(part):
                near = slice(i * LANES, (i + 1) * LANES)
                at = slice((half * part + i) * LANES, (half * part + i + 1) * LANES)
                total = w_ref[0, k:k + 1, at] * moved[off_ref[k, 0] + BAND, :, near]
                for t in range(1, TAPS):
                    total = total + w_ref[t, k:k + 1, at] * moved[off_ref[k, t] + BAND, :, near]
                keep_wide(total, k, near, at, hi_ref, lo_ref, wide_hi, wide_lo)
        if half == 0:
            add_gram(hi_a, lo_a, hh_ref, hl_ref)

    @pl.when(step == steps - 1)
    def _():
        add_gram(hi_b, lo_b, hh_ref, hl_ref)
        finish_gram(hh_ref, hl_ref, pack_ref, scale, core, mine_ref, other_ref)


def gram_v(core, offsets, v, halo, weights, scale):
    cells = v.shape[1]
    half = cells // 2
    tile = min(2048, half)
    steps = half // tile
    ratio = tile // LANES
    last = cells // LANES - 1
    spec = pltpu.PrefetchScalarGridSpec(
        num_scalar_prefetch=2,
        grid=(steps,),
        in_specs=[
            pl.BlockSpec((RANK, tile), lambda i, c, o: (0, c[0] * steps + i)),
            pl.BlockSpec((RANK, LANES), lambda i, c, o: (0, jnp.maximum((c[0] * steps + i) * ratio - 1, 0))),
            pl.BlockSpec((RANK, LANES), lambda i, c, o: (0, jnp.minimum((c[0] * steps + i + 1) * ratio, last))),
            pl.BlockSpec((RANK, LANES), lambda i, c, o: (0, 0)),
            pl.BlockSpec((TAPS, STENCILS, tile), lambda i, c, o: (0, 0, c[0] * steps + i)),
        ],
        out_specs=[pl.BlockSpec((192, LANES), lambda i, c, o: (0, 0))] * 2 + [pl.BlockSpec((WIDE, tile), lambda i, c, o: (0, i))] * 2,
        scratch_shapes=[pltpu.VMEM((2 * BAND + 1, RANK, tile // 2), F32)] * 2 + gram_scratch(tile // 2),
    )
    return pl.pallas_call(
        functools.partial(gram_v_kernel, steps, scale),
        grid_spec=spec,
        out_shape=[jax.ShapeDtypeStruct((192, LANES), F32)] * 2 + [jax.ShapeDtypeStruct((WIDE, half), BF16)] * 2,
        compiler_params=pltpu.CompilerParams(vmem_limit_bytes=VMEM_LIMIT),
        name="gram_v",
    )(core, offsets, v, v, v, halo, weights)


def gram_u_kernel(part_at, parts, steps, scale, core_ref, u_ref, before_ref, after_ref, left_ref, right_ref, m_ref, d_ref, *refs):
    if part_at > 0:
        had_mine, had_other, *refs = refs
    mine_ref, other_ref, hi_a, lo_a, hi_b, lo_b, hh_ref, hl_ref, pack_ref = refs
    step = pl.program_id(0)
    chunks = u_ref.shape[1] // LANES
    part = chunks // 2

    @pl.when(step == 0)
    def _():
        start_gram(hi_b, lo_b, hh_ref, hl_ref)

    before, after = before_ref[...], after_ref[...]
    if part_at == 0:
        before = jnp.where(step == 0, left_ref[...], before)
    if part_at == parts - 1:
        after = jnp.where(step == steps - 1, right_ref[...], after)
    cells = [before] + [u_ref[:, c * LANES:(c + 1) * LANES] for c in range(chunks)] + [after]
    add_gram(hi_b, lo_b, hh_ref, hl_ref)
    for half, hi_ref, lo_ref in ((0, hi_a, lo_a), (1, hi_b, lo_b)):
        for i in range(part):
            c = half * part + i
            near = slice(i * LANES, (i + 1) * LANES)
            at = slice(c * LANES, (c + 1) * LANES)
            up = shift_left(cells[c + 1], cells[c + 2], 1)
            down = shift_right(cells[c], cells[c + 1], 1)
            lap = up - 2.0 * cells[c + 1] + down
            for k in range(STENCILS):
                rows = slice(k * RANK, (k + 1) * RANK)
                hi, lo = split(m_ref[k:k + 1, at] * cells[c + 1] + d_ref[k:k + 1, at] * lap)
                hi_ref[rows, near] = hi
                lo_ref[rows, near] = lo
        if half == 0:
            add_gram(hi_a, lo_a, hh_ref, hl_ref)

    @pl.when(step == steps - 1)
    def _():
        add_gram(hi_b, lo_b, hh_ref, hl_ref)
        finish_gram(hh_ref, hl_ref, pack_ref, scale, core_ref[0], mine_ref, other_ref)
        if part_at > 0:
            mine_ref[...] += had_mine[...]
            other_ref[...] += had_other[...]


def gram_u(core, part_at, parts, u, left, right, mass, diffusion, scale, had=()):
    cells = u.shape[1]
    tile = min(1024, cells // parts)
    steps = cells // parts // tile
    first = part_at * steps
    ratio = tile // LANES
    last = cells // LANES - 1
    table = pl.BlockSpec((STENCILS, tile), lambda i, *_: (0, first + i))
    packed = pl.BlockSpec((192, LANES), lambda i, *_: (0, 0))
    spec = pltpu.PrefetchScalarGridSpec(
        num_scalar_prefetch=1,
        grid=(steps,),
        in_specs=[
            pl.BlockSpec((RANK, tile), lambda i, *_: (0, first + i)),
            pl.BlockSpec((RANK, LANES), lambda i, *_: (0, jnp.maximum((first + i) * ratio - 1, 0))),
            pl.BlockSpec((RANK, LANES), lambda i, *_: (0, jnp.minimum((first + i + 1) * ratio, last))),
            pl.BlockSpec((RANK, LANES), lambda i, *_: (0, 0)),
            pl.BlockSpec((RANK, LANES), lambda i, *_: (0, 0)),
            table,
            table,
        ] + [packed] * len(had),
        out_specs=[packed] * 2,
        scratch_shapes=gram_scratch(tile // 2),
    )
    return pl.pallas_call(
        functools.partial(gram_u_kernel, part_at, parts, steps, scale),
        grid_spec=spec,
        out_shape=[jax.ShapeDtypeStruct((192, LANES), F32)] * 2,
        compiler_params=pltpu.CompilerParams(vmem_limit_bytes=VMEM_LIMIT),
    )(core, u, u, u, left, right, mass, diffusion, *had)


def lower_inverse(square, zero):
    size = RANK
    groups = size // 8
    rows_idx = lax.broadcasted_iota(jnp.int32, (size, size), 0)
    unit = jnp.where(rows_idx == lane_iota((size, size)), 1.0, 0.0).astype(F32)
    both = jnp.concatenate([square, unit], axis=1)
    work = [both[8 * q:8 * q + 8, :] for q in range(groups)]
    shape = (8, 2 * size)
    sub = lax.broadcasted_iota(jnp.int32, shape, 0)

    def lane(x, at):
        return jnp.broadcast_to(x[:, at:at + 1], shape)

    def row(x, at):
        return jnp.broadcast_to(x[at:at + 1, :], shape)

    done = []
    for p in range(groups):
        cols = [lane(work[p], 8 * p + j) + zero for j in range(8)]
        rows = [row(work[p], j) for j in range(8)]
        kept = None
        invs = []
        for j in range(8):
            pivot = row(cols[j], j)
            inv = 1.0 / pivot
            unit_row = rows[j] * lax.rsqrt(pivot)
            kept = unit_row if j == 0 else jnp.where(sub == j, unit_row, kept)
            last = p == groups - 1
            above = cols[j] if last else jnp.where(sub == j, 0.0, cols[j])
            for k in range(j + 1, 8):
                cols[k] = cols[k] - above * (row(cols[j], k) * inv)
            scaled = rows[j] * inv
            for k in range(j + 1 if last else 0, 8):
                if k != j:
                    rows[k] = rows[k] - scaled * row(cols[j], k)
            invs.append(inv)
        if p < groups - 1:
            rows = [r * inv for r, inv in zip(rows, invs)]
        for q in range(p + 1, groups):
            terms = [lane(work[q], 8 * p + j) * rows[j] for j in range(8)]
            while len(terms) > 1:
                terms = [terms[i] + terms[i + 1] for i in range(0, len(terms), 2)]
            work[q] = work[q] - terms[0]
        done.append(kept)
    return jnp.concatenate(done, axis=0)[:, size:]


def unpack(core, mine_ref, other_ref, full_ref):
    first = core == 0
    low = jnp.where(first, mine_ref[...], other_ref[...])
    high = jnp.where(first, other_ref[...], mine_ref[...])
    g10 = jnp.concatenate([low[128:192], high[0:64]], axis=0)
    full_ref[0:128, 0:128] = low[0:128]
    full_ref[128:256, 0:128] = g10
    full_ref[0:128, 128:256] = g10.T
    full_ref[128:256, 128:256] = high[64:192]


def three(x):
    hi, lo = split(x)
    return jnp.concatenate([hi, hi, lo], axis=1)


def put_split(ref, x):
    hi, lo = split(x)
    ref[0:RANK, :] = hi
    ref[RANK:2 * RANK, :] = lo


def chain_kernel(core_ref, gv_mine, gv_other, gu_mine, gu_other, sketch_ref, c_ref, mu_ref, mv_ref, next_ref,
                 gv_ref, gu_ref, panel_ref):
    core = core_ref[0]
    zero = jnp.where(core > 1, 1.0, 0.0).astype(F32)
    unpack(core, gv_mine, gv_other, gv_ref)
    unpack(core, gu_mine, gu_other, gu_ref)
    blocks = [slice(k * RANK, (k + 1) * RANK) for k in range(STENCILS)]
    for k in range(STENCILS):
        panel_ref[k] = gv_ref[:, blocks[k]]
    c = c_ref[...]
    low = lax.broadcasted_iota(jnp.int32, (RANK, RANK), 0) >= lane_iota((RANK, RANK))
    parts = [None] * STENCILS
    w = []
    k_t = None
    for p in range(STENCILS):
        inverse = lower_inverse(panel_ref[p, blocks[p], :], zero)
        below = full_dot(panel_ref[p, p * RANK:, :], inverse, NT)
        for q in range(p + 1, STENCILS):
            head = (q - p) * RANK
            panel_ref[q, q * RANK:, :] -= full_dot(below[head:], below[head:head + RANK], NT)
        for q in range(p, STENCILS):
            head = (q - p) * RANK
            block = below[head:head + RANK]
            if q == p:
                block = jnp.where(low, block, 0.0)
            term = split_dot(sketch_ref[p], block, NT)
            parts[q] = term if parts[q] is None else parts[q] + term
        w.append(split_dot(parts[p], c, NT))
        term = full_dot(w[p], gu_ref[blocks[p], :])
        k_t = term if k_t is None else k_t + term
    w_t = jnp.concatenate(w, axis=1)
    inverse_y = lower_inverse(full_dot(w_t, k_t, NT), zero)
    back = jnp.concatenate([split_dot(k_t[:, at], c) for at in blocks], axis=1)
    back_gram = full_dot(back, gv_ref[...])
    x_t = full_dot(inverse_y, back)
    inner = full_dot(x_t, full_dot(inverse_y, back_gram), NT)
    inverse_c = lower_inverse(inner, zero)
    map_u = split_dot(inverse_y, w_t)
    for k in range(STENCILS):
        mu_ref[blocks[k], :] = three(map_u[:, blocks[k]])
    put_split(mv_ref, split_dot(inverse_c, x_t))
    next_ref[...] = jnp.where(low, full_dot(inner, inverse_c, NT), 0.0)


def chain(core, gv_mine, gv_other, gu_mine, gu_other, sketch_t, core_matrix):
    return pl.pallas_call(
        chain_kernel,
        in_specs=[smem()] + [vmem()] * 6,
        out_specs=[vmem()] * 3,
        out_shape=[
            jax.ShapeDtypeStruct((WIDE, 3 * RANK), BF16),
            jax.ShapeDtypeStruct((2 * RANK, WIDE), BF16),
            jax.ShapeDtypeStruct((RANK, RANK), F32),
        ],
        scratch_shapes=[
            pltpu.VMEM((WIDE, WIDE), F32),
            pltpu.VMEM((WIDE, WIDE), F32),
            pltpu.VMEM((STENCILS, WIDE, RANK), F32),
        ],
        compiler_params=pltpu.CompilerParams(vmem_limit_bytes=VMEM_LIMIT),
        name="chain",
    )(core, gv_mine, gv_other, gu_mine, gu_other, sketch_t, core_matrix)


def next_kernel(map_ref, hi_ref, lo_ref, out_ref):
    both = fast_dot(map_ref[...], hi_ref[...], NN)
    out_ref[...] = both[0:RANK] + (both[RANK:2 * RANK] + fast_dot(map_ref[0:RANK, :], lo_ref[...], NN))


def next_factor(maps, wide_hi, wide_lo):
    cells = wide_hi.shape[1]
    tile = min(2048, cells)
    return pl.pallas_call(
        next_kernel,
        grid=(cells // tile,),
        in_specs=[
            pl.BlockSpec((2 * RANK, WIDE), lambda i: (0, 0)),
            pl.BlockSpec((WIDE, tile), lambda i: (0, i)),
            pl.BlockSpec((WIDE, tile), lambda i: (0, i)),
        ],
        out_specs=pl.BlockSpec((RANK, tile), lambda i: (0, i)),
        out_shape=jax.ShapeDtypeStruct((RANK, cells), F32),
        compiler_params=pltpu.CompilerParams(vmem_limit_bytes=VMEM_LIMIT),
    )(maps, wide_hi, wide_lo)


def next_u_kernel(steps, u_ref, before_ref, after_ref, left_ref, right_ref, m_ref, d_ref, d_before, d_after, map_ref, out_ref,
                  stack, p_ref):
    step = pl.program_id(0)
    chunks = u_ref.shape[1] // LANES
    before = jnp.where(step == 0, left_ref[...], before_ref[...])
    after = jnp.where(step == steps - 1, right_ref[...], after_ref[...])
    cells = [before] + [u_ref[:, c * LANES:(c + 1) * LANES] for c in range(chunks)] + [after]
    for c in range(chunks + 2):
        at = slice(c * LANES, (c + 1) * LANES)
        hi, lo = split(cells[c])
        stack[0:RANK, at] = hi
        stack[RANK:2 * RANK, at] = lo
        stack[2 * RANK:3 * RANK, at] = hi
    p_ref[...] = fast_dot(map_ref[...], stack[...], NN)
    d = [d_before[...]] + [d_ref[:, c * LANES:(c + 1) * LANES] for c in range(chunks)] + [d_after[...]]

    def weighted(c, table):
        total = None
        for k in range(STENCILS):
            term = table[k:k + 1, :] * p_ref[k * RANK:(k + 1) * RANK, c * LANES:(c + 1) * LANES]
            total = term if total is None else total + term
        return total

    pull = [None] + [weighted(c, shift_right(d[c - 1], d[c], 1)) for c in range(1, chunks + 2)]
    push = [weighted(c, shift_left(d[c], d[c + 1], 1)) for c in range(chunks + 1)]
    for c in range(1, chunks + 1):
        at = slice((c - 1) * LANES, c * LANES)
        near = weighted(c, m_ref[:, at] - 2.0 * d[c])
        out_ref[:, at] = near + (shift_left(pull[c], pull[c + 1], 1) + shift_right(push[c - 1], push[c], 1))


def next_u(u, left, right, mass, diffusion, maps):
    cells = u.shape[1]
    tile = min(2048, cells)
    steps = cells // tile
    ratio = tile // LANES
    last = cells // LANES - 1
    table = pl.BlockSpec((STENCILS, tile), lambda i: (0, i))
    low = lambda i: (0, jnp.maximum(i * ratio - 1, 0))
    high = lambda i: (0, jnp.minimum((i + 1) * ratio, last))
    return pl.pallas_call(
        functools.partial(next_u_kernel, steps),
        grid=(steps,),
        in_specs=[
            pl.BlockSpec((RANK, tile), lambda i: (0, i)),
            pl.BlockSpec((RANK, LANES), low),
            pl.BlockSpec((RANK, LANES), high),
            pl.BlockSpec((RANK, LANES), lambda i: (0, 0)),
            pl.BlockSpec((RANK, LANES), lambda i: (0, 0)),
            table,
            table,
            pl.BlockSpec((STENCILS, LANES), low),
            pl.BlockSpec((STENCILS, LANES), high),
            pl.BlockSpec((WIDE, 3 * RANK), lambda i: (0, 0)),
        ],
        out_specs=pl.BlockSpec((RANK, tile), lambda i: (0, i)),
        out_shape=jax.ShapeDtypeStruct((RANK, cells), F32),
        scratch_shapes=[pltpu.VMEM((3 * RANK, tile + 2 * LANES), BF16), pltpu.VMEM((WIDE, tile + 2 * LANES), F32)],
        compiler_params=pltpu.CompilerParams(vmem_limit_bytes=VMEM_LIMIT),
        name="next_u",
    )(u, u, u, left, right, mass, diffusion, diffusion, diffusion, maps)


def make_sketch_t(sketch_seed, wide, rank):
    shape = (wide // rank, rank, rank)
    rows_idx = lax.broadcasted_iota(jnp.int32, shape, 0) * rank + lax.broadcasted_iota(jnp.int32, shape, 2)
    cols_idx = lax.broadcasted_iota(jnp.int32, shape, 1)
    first = (rows_idx * 131 + cols_idx * 977 + sketch_seed[0]) % 65521
    second = first * 7919 % 65521
    upper = second // 256
    lower = second % 256
    third = (upper * upper * 15 + 512 * upper * lower + lower * lower) % 65521
    fourth = (third * 30011 + rows_idx * 17 + cols_idx) % 65521
    return ((fourth.astype(F32) + 0.5) / 65521.0 - 0.5) * 3.4641


def swap(x, axis, bit):
    return lax.ppermute(x, axis, [(i, i ^ bit) for i in range(lax.axis_size(axis))])


def four_way(x, axis, bit):
    near, far, both = (swap(x, axis, b) for b in (bit, 2 * bit, 3 * bit))
    return (x + near) + (far + both)


def body(u, v, mass_table, diffusivity_table, material_index, weights, offsets, core_matrix, sketch_seed):
    gx, pa = lax.axis_size("gx"), lax.axis_size("pa")
    at_gx = lax.axis_index("gx")
    core = (at_gx % 2).astype(jnp.int32).reshape(1)
    even = core[0] == 0
    pairs = []
    for g in range(gx):
        for p in range(pa):
            q = p + 1 if g % 2 == 0 else p - 1
            if 0 <= q < pa:
                pairs.append((g * pa + p, g * pa + q))
    edge_v = jnp.where(even, v[:, -LANES:], v[:, :LANES])
    halo_v = lax.ppermute(edge_v, ("gx", "pa"), pairs)
    onehot = (material_index[:, None, :] == jnp.arange(mass_table.shape[1], dtype=jnp.int32)[None, :, None]).astype(F32)
    mass = jnp.sum(mass_table[:, :, None] * onehot, axis=1)
    diffusion = jnp.sum(diffusivity_table[:, :, None] * onehot, axis=1)
    near_u = swap(jnp.where(even, u[:, -LANES:], u[:, :LANES]), "gx", 1)
    u_pairs = [(i, i - 1 if i % 2 == 0 else i + 1) for i in range(gx)]
    far_u = lax.ppermute(jnp.where(even, u[:, :LANES], u[:, -LANES:]), "gx", [(i, j) for i, j in u_pairs if 0 <= j < gx])
    core_v, mass, diffusion = lax.optimization_barrier((core, mass, diffusion))
    weights = pltpu.with_memory_space_constraint(jnp.transpose(weights, (1, 0, 2)), pltpu.HBM)
    v_in = pltpu.with_memory_space_constraint(v, pltpu.HBM)
    gv_mine, gv_other, hi_v, lo_v = gram_v(core_v, pltpu.with_memory_space_constraint(offsets, pltpu.HBM), v_in, halo_v, weights, 1.0 / (v.shape[1] * pa))
    gv = gv_mine + swap(gv_other, "gx", 1)

    left_u = jnp.where(even, far_u, near_u)
    right_u = jnp.where(even, near_u, far_u)
    u_scale = 1.0 / (u.shape[1] * gx)
    had = gram_u(core, 0, 2, u, left_u, right_u, mass, diffusion, u_scale)
    gu_mine, gu_other = gram_u(core, 1, 2, u, left_u, right_u, mass, diffusion, u_scale, had)
    sketch_t = make_sketch_t(sketch_seed, WIDE, RANK)

    bit = 1
    while bit * 4 < pa:
        gv = gv + swap(gv, "pa", bit)
        bit *= 2
    gu = four_way(gu_mine + swap(gu_other, "gx", 1), "gx", 2)
    gv = four_way(gv, "pa", bit)
    gv_far = swap(gv, "gx", 1)
    gu_far = swap(gu, "gx", 1)
    map_u, map_v, core_next = chain(core, gv, gv_far, gu, gu_far, sketch_t, core_matrix)
    half = next_factor(map_v, hi_v, lo_v)
    half_far = swap(half, "gx", 1)
    u_next = next_u(u, left_u, right_u, mass, diffusion, map_u)
    v_next = jnp.concatenate([jnp.where(even, half, half_far), jnp.where(even, half_far, half)], axis=1)
    return (u_next, v_next, core_next)


def solution(mesh):
    return jax.shard_map(
        body,
        mesh=mesh,
        in_specs=(
            P(None, "gx"),
            P(None, "pa"),
            P(),
            P(),
            P(None, "gx"),
            P(None, None, "pa"),
            P(),
            P(),
            P(),
        ),
        out_specs=(P(None, "gx"), P(None, "pa"), P()),
        check_vma=False,
    )
```
